128 devices in a mesh: lon: 32 (over y, z, x_hi), lat: 4 (over x_lo, core).
Axes of the slice: x: 4 (x_hi: 2, x_lo: 2; x = x_hi * 2 + x_lo), y: 4, z: 4, core: 2. Of those that a mesh axis runs over, the one named last changes fastest.
Arguments:
- spectrum: float32 [1296, 256, 512], P(None, 'lon', 'lat'), may hold values from -6 to 6
- sea_mask: int32 [256, 512], P('lon', 'lat'), may hold values 0 or 1
- transfer: bfloat16 [1296, 1296], replicated, may hold values from -0.15625 to 0.15625
- bulk_weight: float32 [5, 1296], replicated, may hold values from -0.15625 to 0.15625
- remap_cell: int32 [768, 1536, 4], P('lon', 'lat'), may hold values from 0 to 8703, as said below
- remap_weight: float32 [768, 1536, 4], P('lon', 'lat'), may hold values from 0.1 to 0.5
- ocean_u: float32 [8, 768, 1536], P(None, 'lon', 'lat'), may hold values from -6 to 6
- ocean_v: float32 [8, 768, 1536], P(None, 'lon', 'lat'), may hold values from -6 to 6
- ocean_mask: int32 [768, 1536], P('lon', 'lat'), may hold values 0 or 1
- coriolis: float32 [1536], P('lat'), may hold values from -1 to 1
Outputs:
- spectrum_out: float32 [1296, 256, 512], P(None, 'lon', 'lat')
- ocean_u_out: float32 [8, 768, 1536], P(None, 'lon', 'lat')
- ocean_v_out: float32 [8, 768, 1536], P(None, 'lon', 'lat')
The draws below stay inside these ranges and needn't reach their ends.
Inputs may be any that keep to these rules, and one draw needn't show every extreme that they name: `remap_cell`: for ocean cell (i, j) each entry c has c // 512 between 0 and 16, and its wave latitude c % 512 lies in the same block of 128 latitude cells as j // 3.
All inputs are finite; a program needn't handle non-finite values. No bound on the sum of `sea_mask` or of `ocean_mask` on one device may be relied on, other than what follows from the above.
Results may differ from the reference program's by a relative error of at most 0.0016.
Values sent between devices are 32-bit elements; how exact they have to be, the bound alone decides.
A program may use at most 128 MiB of HBM per device.

```python
import jax
import jax.numpy as jnp
from jax import lax

NDIR = 36
NFREQ = 36
K = 1296
WX = 8
WY = 128
LEV = 8
TAPS = 4
NXW = 256
NYW = 512
OXT = 768
OYT = 1536


def draw_remap_cell(key, part):
    key_lon = jax.random.fold_in(key, 11)
    key_lat = jax.random.fold_in(key, 23)
    ocean_lat = jnp.arange(OYT, dtype=jnp.int32)[None, :, None]
    shift_lon = jax.random.randint(key_lon, (OXT, OYT, TAPS), 0, 2 * WX + 1, dtype=jnp.int32)
    shift_lat = jax.random.randint(key_lat, (OXT, OYT, TAPS), -2, 3, dtype=jnp.int32)
    block = ocean_lat // 3 // WY
    wave_lat = jnp.clip(ocean_lat // 3 + shift_lat, block * WY, block * WY + WY - 1)
    return (shift_lon * NYW + wave_lat).astype(jnp.int32)


def plant(values, key, smallest, largest):
    longest = values.shape.index(max(values.shape))
    spots = []
    for shift in (0, 1):
        where = [jax.random.randint(jax.random.fold_in(key, axis), (), 0, length) for axis, length in enumerate(values.shape)]
        where[longest] = (where[longest] + shift) % values.shape[longest]
        spots.append(tuple(where))
    return values.at[spots[0]].set(smallest).at[spots[1]].set(largest)


def steps_of(stream_key, shape, shards, low, high):
    level = 1.0
    for position, blocks in shards:
        steps = jax.random.uniform(jax.random.fold_in(jax.random.fold_in(stream_key, 6), position), (blocks,), jnp.float32, low / len(shards), high / len(shards))
        level = level * jnp.repeat(jnp.exp(steps), shape[position] // blocks).reshape((-1,) + (1,) * (len(shape) - 1 - position))
    return level


def noise(rng, extent, spread, limit, split=(), kind=jnp.bfloat16):
    drawn = spread * jax.random.normal(rng, extent, jnp.float32)
    if split:
        drawn = drawn * steps_of(rng, extent, split, -0.22, 0.18)
    return jnp.clip(drawn, -limit, limit).astype(kind)


def setup_inputs(seed: int = 0) -> dict:
    streams_of = jax.random.split(jax.random.key(seed), 11)
    spectrum = noise(streams_of[0], (K, NXW, NYW), 1.0, 6.0, ((1, 32), (2, 4)), jnp.float32)
    sea_mask = plant((jax.random.randint(streams_of[1], (NXW, NYW), 0, 4) < 3).astype(jnp.int32), jax.random.fold_in(streams_of[1], 1), 0, 1)
    transfer = noise(streams_of[2], (K, K), K ** -0.5, 0.15625)
    bulk_weight = noise(streams_of[3], (5, K), K ** -0.5, 0.15625, (), jnp.float32)
    remap_cell = draw_remap_cell(jax.random.fold_in(streams_of[10], 71), 0)
    remap_weight = jnp.clip(0.1 + 0.4 * jax.random.uniform(streams_of[5], (OXT, OYT, TAPS), jnp.float32) ** steps_of(streams_of[5], (OXT, OYT, TAPS), ((0, 32), (1, 4)), -0.2, 0.2), 0.1, 0.5)
    ocean_u = noise(streams_of[6], (LEV, OXT, OYT), 1.0, 6.0, ((1, 32), (2, 4)), jnp.float32)
    ocean_v = noise(streams_of[7], (LEV, OXT, OYT), 1.0, 6.0, ((1, 32), (2, 4)), jnp.float32)
    ocean_mask = plant((jax.random.randint(streams_of[8], (OXT, OYT), 0, 8) < 7).astype(jnp.int32), jax.random.fold_in(streams_of[8], 1), 0, 1)
    coriolis = jnp.clip(jax.random.uniform(streams_of[9], (OYT,), jnp.float32, -1.0, 1.0) * steps_of(streams_of[9], (OYT,), ((0, 4),), -0.4, 0.0), -1.0, 1.0)
    return dict(spectrum=spectrum, sea_mask=sea_mask, transfer=transfer, bulk_weight=bulk_weight, remap_cell=remap_cell, remap_weight=remap_weight, ocean_u=ocean_u, ocean_v=ocean_v, ocean_mask=ocean_mask, coriolis=coriolis)


def courant():
    index = jnp.arange(NDIR * NFREQ, dtype=jnp.int32)
    direction = (index // NFREQ).astype(jnp.float32)
    level = (index % NFREQ).astype(jnp.float32)
    theta = 2.0 * jnp.pi * (direction + 0.5) / NDIR
    speed = jnp.power(jnp.float32(1.1), -level)
    return (0.45 * speed * jnp.cos(theta))[:, None, None], (0.45 * speed * jnp.sin(theta))[:, None, None]


def advect(extended, east, north):
    centre = extended[:, 1:-1, 1:-1]
    result = (1.0 - jnp.abs(east) - jnp.abs(north)) * centre
    result = result + jnp.maximum(east, 0.0) * extended[:, :-2, 1:-1] + jnp.maximum(-east, 0.0) * extended[:, 2:, 1:-1]
    result = result + jnp.maximum(north, 0.0) * extended[:, 1:-1, :-2] + jnp.maximum(-north, 0.0) * extended[:, 1:-1, 2:]
    return result


def source(advected, transfer, maskf):
    flat = advected.reshape(advected.shape[0], -1).astype(jnp.bfloat16)
    added = jnp.dot(transfer, flat, preferred_element_type=jnp.float32).reshape(advected.shape)
    return maskf * (advected + 0.5 * added)


def ocean_update(padded, ocean_u, ocean_v, drift_u, drift_v, maskf, coriolis):
    levels = ocean_u.shape[0]

    def dxx(q):
        return 0.5 * (q[2:, 1:-1] - q[:-2, 1:-1])

    def dyy(q):
        return 0.5 * (q[1:-1, 2:] - q[1:-1, :-2])

    sxx = padded[2 * levels]
    sxy = padded[2 * levels + 1]
    syy = padded[2 * levels + 2]
    force_x = -(dxx(sxx) + dyy(sxy))
    force_y = -(dxx(sxy) + dyy(syy))

    def laplace(q):
        return q[:, 2:, 1:-1] + q[:, :-2, 1:-1] + q[:, 1:-1, 2:] + q[:, 1:-1, :-2] - 4.0 * q[:, 1:-1, 1:-1]

    decay = jnp.exp(-jnp.arange(levels, dtype=jnp.float32) / 3.0)[:, None, None]
    lap_u = laplace(padded[:levels])
    lap_v = laplace(padded[levels:2 * levels])
    fcor = coriolis[None, None, :]
    new_u = maskf * (ocean_u + 0.5 * fcor * (ocean_v + decay * drift_v) + 0.5 * decay * force_x + 0.1 * lap_u)
    new_v = maskf * (ocean_v - 0.5 * fcor * (ocean_u + decay * drift_u) + 0.5 * decay * force_y + 0.1 * lap_v)
    return new_u, new_v


def pad_grid(field, lon_dim, lat_dim):
    first = lax.slice_in_dim(field, field.shape[lon_dim] - 1, field.shape[lon_dim], axis=lon_dim)
    last = lax.slice_in_dim(field, 0, 1, axis=lon_dim)
    wrapped = jnp.concatenate([first, field, last], axis=lon_dim)
    widths = [(0, 0)] * field.ndim
    widths[lat_dim] = (1, 1)
    return jnp.pad(wrapped, widths)


def reference(spectrum, sea_mask, transfer, bulk_weight, remap_cell, remap_weight, ocean_u, ocean_v, ocean_mask, coriolis):
    east, north = courant()
    maskf = sea_mask.astype(jnp.float32)[None]
    state = spectrum * maskf
    for step in range(2):
        state = source(advect(pad_grid(state, 1, 2), east, north), transfer, maskf)
    flat = state.reshape(state.shape[0], -1)
    bulk = jnp.dot(bulk_weight, flat, precision=lax.Precision.HIGHEST, preferred_element_type=jnp.float32)
    ocean_lon = jnp.arange(OXT, dtype=jnp.int32)[:, None, None]
    wave_lon = (ocean_lon // 3 + remap_cell // NYW - WX + NXW) % NXW
    wave_lat = remap_cell % NYW
    cell = (wave_lon * NYW + wave_lat).astype(jnp.int32)
    taken = jnp.take(bulk, cell.reshape(-1), axis=1).reshape((5,) + remap_cell.shape)
    forcing = jnp.sum(taken * remap_weight[None], axis=-1)
    stacked = jnp.concatenate([ocean_u, ocean_v, forcing[:3]], axis=0)
    padded = pad_grid(stacked, 1, 2)
    new_u, new_v = ocean_update(padded, ocean_u, ocean_v, forcing[3], forcing[4], ocean_mask.astype(jnp.float32)[None], coriolis)
    return state, new_u, new_v
```

```python
import jax
import jax.numpy as jnp
from jax import lax
from jax.experimental import pallas as pl
from jax.experimental.pallas import tpu as pltpu
from jax.sharding import PartitionSpec as P

NFREQ = 36


def passed_along(value, axis, steps):
    count = lax.axis_size(axis)
    first, last = (max(0, -steps), min(count, count - steps))
    return lax.ppermute(value, axis, [(source, source + steps) for source in range(first, last)])


def with_halo(array, sides, width, wrap):
    for axis, dim in sides:
        count, length = (lax.axis_size(axis), array.shape[dim])
        up = [(i, (i + 1) % count) for i in range(count if wrap else count - 1)]
        down = [(j, i) for i, j in up]
        last = lax.slice_in_dim(array, length - width, length, axis=dim)
        first = lax.slice_in_dim(array, 0, width, axis=dim)
        before = lax.ppermute(last, axis, up)
        after = lax.ppermute(first, axis, down)
        array = jnp.concatenate([before, array, after], axis=dim)
    return array


def courant(components, freqs):
    index = jnp.arange(components, dtype=jnp.int32)
    direction = (index // freqs).astype(jnp.float32)
    level = (index % freqs).astype(jnp.float32)
    theta = 2.0 * jnp.pi * (direction + 0.5) / (components // freqs)
    speed = jnp.power(jnp.float32(1.1), -level)
    return (
        (0.45 * speed * jnp.cos(theta))[:, None, None],
        (0.45 * speed * jnp.sin(theta))[:, None, None],
    )


def lat_sides(centre):
    below = passed_along(centre[:, :, -1:], "lat", 1)
    above = passed_along(centre[:, :, :1], "lat", -1)
    return (below, above)


def advect(lon_wide, below, above, east, north):
    centre = lon_wide[:, 1:-1, :]
    south_side = jnp.concatenate([below, centre[:, :, :-1]], axis=2)
    north_side = jnp.concatenate([centre[:, :, 1:], above], axis=2)
    result = (1.0 - jnp.abs(east) - jnp.abs(north)) * centre
    result = (
        result
        + jnp.maximum(east, 0.0) * lon_wide[:, :-2, :]
        + jnp.maximum(-east, 0.0) * lon_wide[:, 2:, :]
    )
    result = result + jnp.maximum(north, 0.0) * south_side + jnp.maximum(-north, 0.0) * north_side
    return result


def source(advected, transfer, maskf):
    flat = advected.reshape(advected.shape[0], -1).astype(jnp.bfloat16)
    added = jnp.dot(transfer, flat, preferred_element_type=jnp.float32).reshape(advected.shape)
    return maskf * (advected + 0.5 * added)


def ocean_update(padded, ocean_u, ocean_v, drift_u, drift_v, maskf, coriolis):
    levels = ocean_u.shape[0]

    def dxx(q):
        return 0.5 * (q[2:, 1:-1] - q[:-2, 1:-1])

    def dyy(q):
        return 0.5 * (q[1:-1, 2:] - q[1:-1, :-2])

    sxx = padded[2 * levels]
    sxy = padded[2 * levels + 1]
    syy = padded[2 * levels + 2]
    force_x = -(dxx(sxx) + dyy(sxy))
    force_y = -(dxx(sxy) + dyy(syy))

    def laplace(q):
        return (
            q[:, 2:, 1:-1]
            + q[:, :-2, 1:-1]
            + q[:, 1:-1, 2:]
            + q[:, 1:-1, :-2]
            - 4.0 * q[:, 1:-1, 1:-1]
        )

    decay = jnp.exp(-jnp.arange(levels, dtype=jnp.float32) / 3.0)[:, None, None]
    lap_u = laplace(padded[:levels])
    lap_v = laplace(padded[levels : 2 * levels])
    fcor = coriolis[None, None, :]
    new_u = maskf * (
        ocean_u + 0.5 * fcor * (ocean_v + decay * drift_v) + 0.5 * decay * force_x + 0.1 * lap_u
    )
    new_v = maskf * (
        ocean_v - 0.5 * fcor * (ocean_u + decay * drift_u) + 0.5 * decay * force_y + 0.1 * lap_v
    )
    return (new_u, new_v)


def remap_kernel(near_ref, cell_ref, weight_ref, out_ref, near3, cells, weights):
    quantities, columns, lanes = near_ref.shape
    rows, taps, width = cell_ref.shape
    for i in range(columns):
        for q in range(quantities):
            near3[q, pl.ds(3 * i, 3), :] = jnp.broadcast_to(near_ref[q, pl.ds(i, 1), :], (3, lanes))
    for i in range(rows):
        for t in range(taps):
            cells[t, pl.ds(i, 1), :] = cell_ref[i, pl.ds(t, 1), :]
            weights[t, pl.ds(i, 1), :] = weight_ref[i, pl.ds(t, 1), :]

    def block(jb, carry):
        lane = pl.multiple_of(jb * lanes, lanes)
        for i0 in range(0, rows, 8):
            codes = [cells[t, pl.ds(i0, 8), pl.ds(lane, lanes)] for t in range(taps)]
            places = [c & (lanes - 1) for c in codes]
            offsets = [c >> 9 for c in codes]
            taken = [[jnp.zeros((8, lanes), jnp.float32)] * quantities for t in range(taps)]
            for o in range(17):
                hits = [offset == o for offset in offsets]
                for q in range(quantities):
                    source = near3[q, pl.ds(i0 + 3 * o, 8), :]
                    for t in range(taps):
                        got = jnp.take_along_axis(source, places[t], axis=1, mode="promise_in_bounds")
                        taken[t][q] = jnp.where(hits[t], got, taken[t][q])
            for q in range(quantities):
                total = 0.0
                for t in range(taps):
                    total = total + taken[t][q] * weights[t, pl.ds(i0, 8), pl.ds(lane, lanes)]
                out_ref[q, pl.ds(i0, 8), pl.ds(lane, lanes)] = total
        return carry

    lax.fori_loop(0, width // lanes, block, 0)


def remapped(near, cell, weight):
    quantities, columns, lanes = near.shape
    rows, taps, width = cell.shape
    return pl.pallas_call(
        remap_kernel,
        out_shape=jax.ShapeDtypeStruct((quantities, rows, width), jnp.float32),
        in_specs=[pl.BlockSpec(memory_space=pltpu.VMEM)] * 3,
        out_specs=pl.BlockSpec(memory_space=pltpu.VMEM),
        scratch_shapes=[
            pltpu.VMEM((quantities, 3 * columns, lanes), jnp.float32),
            pltpu.VMEM((taps, rows, width), jnp.int32),
            pltpu.VMEM((taps, rows, width), jnp.float32),
        ],
    )(near, cell, weight)


def local(
    spectrum,
    sea_mask,
    transfer,
    bulk_weight,
    remap_cell,
    remap_weight,
    ocean_u,
    ocean_v,
    ocean_mask,
    coriolis,
):
    components, width_x, width_y = spectrum.shape
    east, north = courant(components, NFREQ)
    maskf = sea_mask.astype(jnp.float32)[None]
    state = spectrum * maskf
    for step in range(2):
        extended = with_halo(state, (("lon", 1),), 1, True)
        below, above = lat_sides(state)
        state = source(advect(extended, below, above, east, north), transfer, maskf)
    flat = state.reshape(components, -1)
    bulk = jnp.dot(
        bulk_weight, flat, precision=lax.Precision.HIGHEST, preferred_element_type=jnp.float32
    )
    bulk = bulk.reshape(5, width_x, width_y)
    near = with_halo(bulk, (("lon", 1),), width_x, True)
    forcing = remapped(
        near, jnp.transpose(remap_cell, (0, 2, 1)), jnp.transpose(remap_weight, (0, 2, 1))
    )
    stacked = jnp.concatenate([ocean_u, ocean_v, forcing[:3]], axis=0)
    padded = with_halo(stacked, (("lon", 1),), 1, True)
    padded = with_halo(padded, (("lat", 2),), 1, False)
    new_u, new_v = ocean_update(
        padded,
        ocean_u,
        ocean_v,
        forcing[3],
        forcing[4],
        ocean_mask.astype(jnp.float32)[None],
        coriolis,
    )
    return (state, new_u, new_v)


def solution(mesh):
    placed = (
        P(None, "lon", "lat"),
        P("lon", "lat"),
        P(),
        P(),
        P("lon", "lat", None),
        P("lon", "lat", None),
        P(None, "lon", "lat"),
        P(None, "lon", "lat"),
        P("lon", "lat"),
        P("lat"),
    )
    return jax.shard_map(
        local,
        mesh=mesh,
        in_specs=placed,
        out_specs=(P(None, "lon", "lat"), P(None, "lon", "lat"), P(None, "lon", "lat")),
        check_vma=False,
    )
```

```python
import math

import jax
import jax.numpy as jnp
from jax import lax
from jax.experimental import pallas as pl
from jax.experimental.pallas import tpu as pltpu
from jax.sharding import PartitionSpec as P

NFREQ = 36
MESH = pl.DeviceIdType.MESH
VMEM = pl.BlockSpec(memory_space=pltpu.VMEM)
ANY = pl.BlockSpec(memory_space=pl.ANY)
LANES = 128
PAIR = 16
GRANT = 60 * 1024 * 1024


def courant(components, freqs):
    index = jnp.arange(components, dtype=jnp.int32)
    direction = (index // freqs).astype(jnp.float32)
    level = (index % freqs).astype(jnp.float32)
    theta = 2.0 * jnp.pi * (direction + 0.5) / (components // freqs)
    speed = jnp.power(jnp.float32(1.1), -level)
    east = 0.45 * speed * jnp.cos(theta)
    north = 0.45 * speed * jnp.sin(theta)
    return jnp.stack(
        [
            1.0 - jnp.abs(east) - jnp.abs(north),
            jnp.abs(east),
            jnp.abs(north),
            jnp.maximum(east, 0.0),
            jnp.maximum(-east, 0.0),
            jnp.maximum(north, 0.0),
            jnp.maximum(-north, 0.0),
            jnp.zeros_like(east),
        ],
        axis=1,
    )


def sign_of(function, first, last, freqs, directions):
    signs = set()
    for d in range(first // freqs, (last - 1) // freqs + 1):
        signs.add(1 if function(2 * math.pi * (d + 0.5) / directions) > 0 else -1)
    return signs.pop() if len(signs) == 1 else 0


def segments(components, freqs):
    directions = components // freqs
    runs = []
    for pair in range(components // PAIR):
        first, last = pair * PAIR, (pair + 1) * PAIR
        key = (
            sign_of(math.cos, first, last, freqs, directions),
            sign_of(math.sin, first, last, freqs, directions),
        )
        if runs and runs[-1][2] == key:
            runs[-1][1] = pair + 1
        else:
            runs.append([pair, pair + 1, key])
    return [(a, b, xs, ys) for a, b, (xs, ys) in runs]


def row_spans(components, freqs, sign):
    spans = []
    for a, b, xs, _ in segments(components, freqs):
        if xs == -sign:
            continue
        if spans and spans[-1][1] == a * PAIR:
            spans[-1][1] = b * PAIR
        else:
            spans.append([a * PAIR, b * PAIR])
    return [tuple(s) for s in spans]


def complement(spans, total):
    out, at = [], 0
    for a, b in spans:
        if a > at:
            out.append((at, a))
        at = b
    if at < total:
        out.append((at, total))
    return out


def south_lane(c):
    return 2 * c + 1 if 0 <= c < 8 else (32 if c < 0 else 33)


def north_lane(c):
    return 16 + 2 * c if 0 <= c < 8 else (34 if c < 0 else 35)


def lane_shift(x, source, target):
    return pltpu.roll(x, (target - source) % LANES, 1)


def coefficients(coef, xs, ys):
    def wide(n):
        return jnp.broadcast_to(coef[:, n : n + 1], (PAIR, LANES))

    return dict(
        c=wide(0),
        x=wide(1) if xs else (wide(3), wide(4)),
        y=wide(2) if ys else (wide(5), wide(6)),
    )


def upwind(co, xs, ys, centre, west, east, south, north):
    result = co["c"] * centre
    if xs:
        result = result + co["x"] * (west() if xs > 0 else east())
    else:
        result = result + co["x"][0] * west() + co["x"][1] * east()
    if ys:
        result = result + co["y"] * (south() if ys > 0 else north())
    else:
        result = result + co["y"][0] * south() + co["y"][1] * north()
    return result


def advect_columns(co, xs, ys, columns, state, ghost, lane):
    out = {}
    for c in columns:
        out[c] = upwind(
            co,
            xs,
            ys,
            state[c],
            lambda: state[c - 1],
            lambda: state[c + 1],
            lambda: jnp.where(
                lane == 0, lane_shift(ghost, south_lane(c), 0), pltpu.roll(state[c], 1, 1)
            ),
            lambda: jnp.where(
                lane == LANES - 1,
                lane_shift(ghost, north_lane(c), LANES - 1),
                pltpu.roll(state[c], LANES - 1, 1),
            ),
        )
    return out


def needed(columns, xs):
    want = set(columns)
    if xs >= 0:
        want |= {c - 1 for c in columns}
    if xs <= 0:
        want |= {c + 1 for c in columns}
    return sorted(want)


def over_rows(runs, body):
    for a, b, xs, ys in runs:
        if b - a == 1:
            body(a * PAIR, xs, ys)
        else:
            def step(p, carry, xs=xs, ys=ys):
                body(pl.multiple_of(p * PAIR, PAIR), xs, ys)
                return carry

            lax.fori_loop(a, b, step, 0)


def wave_kernel(
    spectrum, sea, transfer, coef_hbm, cell_hbm, weight_hbm, u_hbm, v_hbm,
    x1_out, ghost_out, cells_out, weights_out, rows_out, cols_out,
    x, a, ab, abe, t, coef, masks, sides, packed, turned, gturned, g, ga,
    cell, weight, u, v, cells, weights, rows_send, cols_send, rows_in, cols_in,
    local_sem, send_sem, recv_sem, out_sem,
):
    lon, lat = lax.axis_index("lon"), lax.axis_index("lat")
    nlon, nlat = lax.axis_size("lon"), lax.axis_size("lat")
    components, width, _ = spectrum.shape
    runs = segments(components, NFREQ)
    plus = row_spans(components, NFREQ, 1)
    minus = row_spans(components, NFREQ, -1)
    east, west = lax.rem(lon + 1, nlon), lax.rem(lon + nlon - 1, nlon)
    has_south, has_north = lat > 0, lat < nlat - 1
    lane = lax.broadcasted_iota(jnp.int32, (PAIR, LANES), 1)

    gturned[...] = jnp.zeros_like(gturned)
    cols_in[...] = jnp.zeros_like(cols_in)

    local = []

    def load(src, dst):
        copy = pltpu.make_async_copy(src, dst, local_sem.at[len(local)])
        copy.start()
        local.append(copy)
        return copy

    barrier = pltpu.get_barrier_semaphore()

    def greet(to_lon, to_lat):
        pl.semaphore_signal(barrier, inc=1, device_id=(to_lon, to_lat), device_id_type=MESH)

    greet(east, lat)
    greet(west, lat)

    @pl.when(has_north)
    def _():
        greet(lon, lat + 1)
        greet(east, lat + 1)
        greet(west, lat + 1)

    @pl.when(has_south)
    def _():
        greet(lon, lat - 1)
        greet(east, lat - 1)
        greet(west, lat - 1)

    columns_in = [load(spectrum.at[:, c, :], x.at[c + 2]) for c in range(width)]
    coef_in = load(coef_hbm, coef)
    cell_in = load(cell_hbm, cell)
    weight_in = load(weight_hbm, weight)
    u_in = load(u_hbm, u)
    v_in = load(v_hbm, v)
    transfer_in = load(transfer, t)

    pl.semaphore_wait(
        barrier, 2 + 3 * has_north.astype(jnp.int32) + 3 * has_south.astype(jnp.int32)
    )

    count = [0]

    def remote(src, dst, to_lon, to_lat):
        n = count[0]
        count[0] += 1
        return pltpu.make_async_remote_copy(
            src_ref=src,
            dst_ref=dst,
            send_sem=send_sem.at[n],
            recv_sem=recv_sem.at[n],
            device_id=(to_lon, to_lat),
            device_id_type=MESH,
        )

    def columns(spans, column, slot, to_lon):
        return [
            remote(
                spectrum.at[pl.ds(k0, k1 - k0), column, :],
                x.at[slot, pl.ds(k0, k1 - k0), :],
                to_lon,
                lat,
            )
            for k0, k1 in spans
        ]

    first = columns(plus, width - 1, 1, east) + columns(minus, 0, width + 2, west)
    second = (
        columns(complement(plus, components), width - 1, 1, east)
        + columns(plus, width - 2, 0, east)
        + columns(complement(minus, components), 0, width + 2, west)
        + columns(minus, 1, width + 3, west)
    )
    side_masks = [remote(sea, sides.at[0], east, lat), remote(sea, sides.at[1], west, lat)]
    for copy in side_masks + first:
        copy.start()

    for c in range(width):
        masks[c + 2] = jnp.broadcast_to(
            sea[pl.ds(c, 1), :].astype(jnp.float32), (PAIR, LANES)
        )

    for copy in columns_in:
        copy.wait()

    def pack(r, values):
        total = jnp.zeros((PAIR, LANES), jnp.float32)
        half = lane // 2
        for c in range(width):
            total = jnp.where(half == c, lane_shift(values[c], LANES - 2, 2 * c), total)
            total = jnp.where(half == 8 + c, lane_shift(values[c], 0, 16 + 2 * c), total)
        packed[pl.ds(r, PAIR), :] = total

    def pack_rows(p, carry):
        r = pl.multiple_of(p * PAIR, PAIR)
        pack(r, [x[c + 2, pl.ds(r, PAIR), :] * masks[c + 2] for c in range(width)])
        return carry

    lax.fori_loop(0, components // PAIR, pack_rows, 0)
    pack(components, [masks[c + 2] for c in range(width)])
    blocks = packed.shape[0] // LANES
    tail = components + PAIR
    packed[pl.ds(tail, blocks * LANES - tail), :] = jnp.zeros(
        (blocks * LANES - tail, LANES), jnp.float32
    )
    for b in range(blocks):
        turned[:, b * LANES : (b + 1) * LANES] = jnp.transpose(
            packed[b * LANES : (b + 1) * LANES, :]
        )[:32, :]

    for copy in (cell_in, weight_in, u_in, v_in):
        copy.wait()
    height, taps, length = cell.shape
    for i in range(height):
        for tap in range(taps):
            cells[tap, pl.ds(i, 1), :] = cell[i, pl.ds(tap, 1), :]
            weights[tap, pl.ds(i, 1), :] = weight[i, pl.ds(tap, 1), :]
    levels = u.shape[0]
    for side, row in ((0, height - 1), (1, 0)):
        for level in range(levels):
            rows_send[side, pl.ds(level, 1), :] = u[level, pl.ds(row, 1), :]
            rows_send[side, pl.ds(levels + level, 1), :] = v[level, pl.ds(row, 1), :]
        for tap in range(taps):
            rows_send[side, pl.ds(2 * levels + tap, 1), :] = weights[tap, pl.ds(row, 1), :]
            rows_send[side, pl.ds(2 * levels + taps + tap, 1), :] = cells[
                tap, pl.ds(row, 1), :
            ].astype(jnp.float32)
    lane_all = lax.broadcasted_iota(jnp.int32, (height, LANES), 1)
    for side, start, source in ((0, length - LANES, LANES - 1), (1, 0, 0)):
        total = jnp.zeros((height, LANES), jnp.float32)
        for n in range(2 * levels + 2 * taps):
            if n < levels:
                block = u[n, :, start : start + LANES]
            elif n < 2 * levels:
                block = v[n - levels, :, start : start + LANES]
            elif n < 2 * levels + taps:
                block = weights[n - 2 * levels, :, start : start + LANES]
            else:
                block = cells[n - 2 * levels - taps, :, start : start + LANES].astype(jnp.float32)
            total = jnp.where(lane_all == n, lane_shift(block, source, n), total)
        cols_send[side] = total

    rows_copy = [
        remote(rows_send.at[0], rows_in.at[0], east, lat),
        remote(rows_send.at[1], rows_in.at[1], west, lat),
    ]
    to_north = [
        remote(turned.at[pl.ds(0, 16), :], gturned.at[pl.ds(0, 16), :], lon, lat + 1),
        remote(turned.at[pl.ds(15, 1), :], gturned.at[pl.ds(32, 1), :], east, lat + 1),
        remote(turned.at[pl.ds(1, 1), :], gturned.at[pl.ds(33, 1), :], west, lat + 1),
        remote(cols_send.at[0], cols_in.at[0], lon, lat + 1),
    ]
    to_south = [
        remote(turned.at[pl.ds(16, 16), :], gturned.at[pl.ds(16, 16), :], lon, lat - 1),
        remote(turned.at[pl.ds(30, 1), :], gturned.at[pl.ds(34, 1), :], east, lat - 1),
        remote(turned.at[pl.ds(16, 1), :], gturned.at[pl.ds(35, 1), :], west, lat - 1),
        remote(cols_send.at[1], cols_in.at[1], lon, lat - 1),
    ]

    @pl.when(has_north)
    def _():
        for copy in to_north:
            copy.start()

    @pl.when(has_south)
    def _():
        for copy in to_south:
            copy.start()

    for copy in rows_copy + second:
        copy.start()

    stores = []

    def store(src, dst):
        copy = pltpu.make_async_copy(src, dst, out_sem.at[len(stores)])
        copy.start()
        stores.append(copy)

    store(cells, cells_out)
    store(weights, weights_out)

    for copy in side_masks + first:
        copy.wait_recv()

    @pl.when(has_south)
    def _():
        for copy in to_north:
            copy.wait_recv()

    @pl.when(has_north)
    def _():
        for copy in to_south:
            copy.wait_recv()

    for slot, side, row in ((0, 0, width - 2), (1, 0, width - 1), (width + 2, 1, 0), (width + 3, 1, 1)):
        masks[slot] = jnp.broadcast_to(
            sides[side, pl.ds(row, 1), :].astype(jnp.float32), (PAIR, LANES)
        )
    for b in range(blocks):
        g[b * LANES : (b + 1) * LANES, :] = jnp.transpose(
            gturned[:, b * LANES : (b + 1) * LANES]
        )
    coef_in.wait()
    own = list(range(width))

    def first_step(r, xs, ys):
        co = coefficients(coef[pl.ds(r, PAIR), :], xs, ys)
        state = {c: x[c + 2, pl.ds(r, PAIR), :] * masks[c + 2] for c in needed(own, xs)}
        ghost = g[pl.ds(r, PAIR), :]
        mine = packed[pl.ds(r, PAIR), :]
        for c, value in advect_columns(co, xs, ys, own, state, ghost, lane).items():
            a[c + 1, pl.ds(r, PAIR), :] = value
            ab[pl.ds(r, PAIR), c * LANES : (c + 1) * LANES] = value.astype(jnp.bfloat16)

        def sideways(step, low, high):
            moved = pltpu.roll(ghost, step % LANES, 1)
            for target, source in (low, high):
                moved = jnp.where(lane == target, lane_shift(ghost, source, target), moved)
            return moved

        value = upwind(
            co,
            xs,
            ys,
            ghost,
            lambda: sideways(2, (1, 32), (16, 34)),
            lambda: sideways(-2, (15, 33), (30, 35)),
            lambda: jnp.where(lane < 16, pltpu.roll(ghost, 1, 1), pltpu.roll(mine, 15, 1)),
            lambda: jnp.where(
                lane < 16, pltpu.roll(mine, LANES - 15, 1), pltpu.roll(ghost, LANES - 1, 1)
            ),
        )
        ga[pl.ds(r, PAIR), :] = value
        ab[pl.ds(r, PAIR), width * LANES : (width + 1) * LANES] = value.astype(jnp.bfloat16)

    over_rows(runs, first_step)
    transfer_in.wait()
    block = 432
    ghost_mask = g[pl.ds(components, 1), :]

    def product(m, carry):
        r = pl.multiple_of(m * block, PAIR)
        rows = pl.ds(r, block)
        for n in range(0, width, 2):
            added = jnp.dot(
                t[rows, :],
                ab[:, n * LANES : (n + 2) * LANES],
                preferred_element_type=jnp.float32,
            )
            for c in (n, n + 1):
                part = added[:, (c - n) * LANES : (c - n + 1) * LANES]
                a[c + 1, rows, :] = masks[c + 2, pl.ds(0, 1), :] * (a[c + 1, rows, :] + 0.5 * part)
        added = jnp.dot(
            t[rows, :],
            ab[:, width * LANES : (width + 1) * LANES],
            preferred_element_type=jnp.float32,
        )
        ga[rows, :] = ghost_mask * (ga[rows, :] + 0.5 * added)
        return carry

    lax.fori_loop(0, components // block, product, 0)
    for c in range(width):
        store(a.at[c + 1], x1_out.at[c + 1])
    store(ga, ghost_out)

    for copy in rows_copy + second:
        copy.wait_recv()
    store(rows_in, rows_out)
    store(cols_in, cols_out)

    outer = [-1, width]

    def outer_step(r, xs, ys):
        co = coefficients(coef[pl.ds(r, PAIR), :], xs, ys)
        state = {c: x[c + 2, pl.ds(r, PAIR), :] * masks[c + 2] for c in needed(outer, xs)}
        ghost = g[pl.ds(r, PAIR), :]
        for c, value in advect_columns(co, xs, ys, outer, state, ghost, lane).items():
            slot = 0 if c < 0 else 1
            a[c + 1, pl.ds(r, PAIR), :] = value
            abe[pl.ds(r, PAIR), slot * LANES : (slot + 1) * LANES] = value.astype(jnp.bfloat16)

    over_rows(runs, outer_step)
    for slot, c, spans in ((0, -1, plus), (1, width, minus)):
        for k0, k1 in spans:
            rows = pl.ds(k0, k1 - k0)
            added = jnp.dot(
                t[rows, :],
                abe[:, slot * LANES : (slot + 1) * LANES],
                preferred_element_type=jnp.float32,
            )
            a[c + 1, rows, :] = masks[c + 2, pl.ds(0, 1), :] * (a[c + 1, rows, :] + 0.5 * added)
            store(a.at[c + 1, rows, :], x1_out.at[c + 1, rows, :])

    for copy in side_masks + first + rows_copy + second:
        copy.wait_send()

    @pl.when(has_north)
    def _():
        for copy in to_north:
            copy.wait_send()

    @pl.when(has_south)
    def _():
        for copy in to_south:
            copy.wait_send()

    for copy in stores:
        copy.wait()


def second_kernel(
    x1_hbm, ghost_hbm, sea, transfer, coef_hbm, bulk_hbm, out, bulk_ref,
    x, a, ab, t, coef, bulk_weight, g, local_sem, out_sem,
):
    width = sea.shape[0]
    components = coef.shape[0]
    runs = segments(components, NFREQ)
    lane = lax.broadcasted_iota(jnp.int32, (PAIR, LANES), 1)
    local = []

    def load(src, dst):
        copy = pltpu.make_async_copy(src, dst, local_sem.at[len(local)])
        copy.start()
        local.append(copy)

    load(coef_hbm, coef)
    load(ghost_hbm, g)
    for c in range(-1, width + 1):
        if c < 0 or c == width:
            for k0, k1 in row_spans(components, NFREQ, 1 if c < 0 else -1):
                rows = pl.ds(k0, k1 - k0)
                load(x1_hbm.at[c + 1, rows, :], x.at[c + 1, rows, :])
        else:
            load(x1_hbm.at[c + 1], x.at[c + 1])
    waits = list(local)
    load(transfer, t)
    load(bulk_hbm, bulk_weight)
    for copy in waits:
        copy.wait()
    own = list(range(width))

    def step(r, xs, ys):
        co = coefficients(coef[pl.ds(r, PAIR), :], xs, ys)
        state = {c: x[c + 1, pl.ds(r, PAIR), :] for c in needed(own, xs)}
        ghost = g[pl.ds(r, PAIR), :]
        for c, value in advect_columns(co, xs, ys, own, state, ghost, lane).items():
            a[c, pl.ds(r, PAIR), :] = value
            ab[pl.ds(r, PAIR), c * LANES : (c + 1) * LANES] = value.astype(jnp.bfloat16)

    over_rows(runs, step)
    for copy in local[len(waits) :]:
        copy.wait()
    block = 432
    stores = []
    for m in range(components // block):
        rows = pl.ds(m * block, block)
        for n in range(0, width, 2):
            added = jnp.dot(
                t[rows, :],
                ab[:, n * LANES : (n + 2) * LANES],
                preferred_element_type=jnp.float32,
            )
            for c in (n, n + 1):
                part = added[:, (c - n) * LANES : (c - n + 1) * LANES]
                wet = sea[pl.ds(c, 1), :].astype(jnp.float32)
                a[c, rows, :] = wet * (a[c, rows, :] + 0.5 * part)
        for c in range(width):
            copy = pltpu.make_async_copy(
                a.at[c, rows, :], out.at[rows, c, :], out_sem.at[len(stores)]
            )
            copy.start()
            stores.append(copy)
    quantities = bulk_ref.shape[0]
    half = width // 2
    for c0 in range(0, width, half):

        def gather(k, totals):
            r = pl.multiple_of(k * 8, 8)
            line = bulk_weight[pl.ds(r, 8), :]
            totals = list(totals)
            wide = [jnp.broadcast_to(line[:, q : q + 1], (8, LANES)) for q in range(quantities)]
            for c in range(half):
                state = a[c0 + c, pl.ds(r, 8), :]
                for q in range(quantities):
                    totals[c * quantities + q] = totals[c * quantities + q] + wide[q] * state
            return tuple(totals)

        zero = jnp.zeros((8, LANES), jnp.float32)
        totals = lax.fori_loop(0, components // 8, gather, (zero,) * (half * quantities))
        for c in range(half):
            for q in range(quantities):
                bulk_ref[q, pl.ds(c0 + c, 1), :] = jnp.sum(
                    totals[c * quantities + q], axis=0, keepdims=True
                )
    for copy in stores:
        copy.wait()


def spread_kernel(bulk, near_out, sides_out, far_out, send_sem, recv_sem):
    lon, lat = lax.axis_index("lon"), lax.axis_index("lat")
    nlon, nlat = lax.axis_size("lon"), lax.axis_size("lat")
    around = [lax.rem(lon + d + nlon, nlon) for d in (-2, -1, 0, 1, 2)]
    has_south, has_north = lat > 0, lat < nlat - 1
    sides_out[...] = jnp.zeros_like(sides_out)
    barrier = pltpu.get_barrier_semaphore()

    def greet(to_lon, to_lat):
        pl.semaphore_signal(barrier, inc=1, device_id=(to_lon, to_lat), device_id_type=MESH)

    for d in (0, 1, 3, 4):
        greet(around[d], lat)

    @pl.when(has_north)
    def _():
        for d in (1, 2, 3):
            greet(around[d], lat + 1)

    @pl.when(has_south)
    def _():
        for d in (1, 2, 3):
            greet(around[d], lat - 1)

    pl.semaphore_wait(
        barrier, 4 + 3 * has_north.astype(jnp.int32) + 3 * has_south.astype(jnp.int32)
    )
    count = [0]

    def remote(src, dst, to_lon, to_lat):
        n = count[0]
        count[0] += 1
        return pltpu.make_async_remote_copy(
            src_ref=src,
            dst_ref=dst,
            send_sem=send_sem.at[n],
            recv_sem=recv_sem.at[n],
            device_id=(to_lon, to_lat),
            device_id_type=MESH,
        )

    drift = bulk.at[pl.ds(1, 2)]
    stress = bulk.at[pl.ds(0, 2)]
    flat = [
        remote(bulk, near_out.at[2], around[1], lat),
        remote(bulk, near_out.at[0], around[3], lat),
        remote(stress, far_out.at[1], around[0], lat),
        remote(stress, far_out.at[0], around[4], lat),
    ]
    to_north = [
        remote(drift, sides_out.at[0, 2], around[1], lat + 1),
        remote(drift, sides_out.at[0, 1], around[2], lat + 1),
        remote(drift, sides_out.at[0, 0], around[3], lat + 1),
    ]
    to_south = [
        remote(drift, sides_out.at[1, 2], around[1], lat - 1),
        remote(drift, sides_out.at[1, 1], around[2], lat - 1),
        remote(drift, sides_out.at[1, 0], around[3], lat - 1),
    ]
    for copy in flat:
        copy.start()

    @pl.when(has_north)
    def _():
        for copy in to_north:
            copy.start()

    @pl.when(has_south)
    def _():
        for copy in to_south:
            copy.start()

    near_out[1] = bulk[...]

    for copy in flat:
        copy.wait()

    @pl.when(has_north)
    def _():
        for copy in to_north:
            copy.wait_send()
        for copy in to_south:
            copy.wait_recv()

    @pl.when(has_south)
    def _():
        for copy in to_south:
            copy.wait_send()
        for copy in to_north:
            copy.wait_recv()


def taken_from(sources, codes, quantities):
    places = [c & (LANES - 1) for c in codes]
    offsets = [c >> 9 for c in codes]
    taken = [[jnp.zeros(codes[0].shape, jnp.float32)] * len(quantities) for _ in codes]
    for o in range(17):
        hits = [offset == o for offset in offsets]
        for n, q in enumerate(quantities):
            source = sources(q, o)
            for i in range(len(codes)):
                got = jnp.take_along_axis(source, places[i], axis=1, mode="promise_in_bounds")
                taken[i][n] = jnp.where(hits[i], got, taken[i][n])
    return taken


def ocean_kernel(
    near, sides, far, cells, weights, rows_in, cols_in, u, v, sea, coriolis, u_out, v_out,
    near1, near3, sides3, forcing, edge_code, edge_weight, edge_rows,
):
    quantities = near.shape[1]
    width = near.shape[2]
    taps, height, length = cells.shape
    levels = u.shape[0]
    for part in range(3):
        near1[:, pl.ds(8 + part * width, width), :] = near[part]
    near1[pl.ds(0, 2), pl.ds(7, 1), :] = far[0, :, pl.ds(width - 1, 1), :]
    near1[pl.ds(0, 2), pl.ds(8 + 3 * width, 1), :] = far[1, :, pl.ds(0, 1), :]
    for i in range(3 * width):
        for q in range(quantities):
            near3[q, pl.ds(3 * i, 3), :] = jnp.broadcast_to(
                near1[q, pl.ds(8 + i, 1), :], (3, LANES)
            )
        for side in range(2):
            for q in range(2):
                sides3[side, q, pl.ds(3 * i, 3), :] = jnp.broadcast_to(
                    sides[side, i // width, q, pl.ds(i % width, 1), :], (3, LANES)
                )

    def block(jb, carry):
        lanes = pl.ds(pl.multiple_of(jb * LANES, LANES), LANES)
        for i0 in range(0, height, 8):
            rows = pl.ds(i0, 8)
            taken = taken_from(
                lambda q, o: near3[q, pl.ds(i0 + 3 * o, 8), :],
                [cells[tap, rows, lanes] for tap in range(taps)],
                range(quantities),
            )
            for q in range(quantities):
                total = 0.0
                for tap in range(taps):
                    total = total + taken[tap][q] * weights[tap, rows, lanes]
                forcing[q, rows, lanes] = total
        low = lax.broadcasted_iota(jnp.int32, (8, LANES), 0) < 4
        taken = taken_from(
            lambda q, o: jnp.where(
                low,
                jnp.broadcast_to(near1[q, pl.ds(7 + o, 1), :], (8, LANES)),
                jnp.broadcast_to(near1[q, pl.ds(16 + o, 1), :], (8, LANES)),
            ),
            [edge_code[:, lanes].astype(jnp.int32)],
            range(2),
        )
        for q in range(2):
            product = taken[0][q] * edge_weight[:, lanes]
            zero = jnp.zeros_like(product)
            edge_rows[q, pl.ds(0, 1), lanes] = jnp.sum(
                jnp.where(low, product, zero), axis=0, keepdims=True
            )
            edge_rows[q, pl.ds(1, 1), lanes] = jnp.sum(
                jnp.where(low, zero, product), axis=0, keepdims=True
            )
        return carry

    for side in range(2):
        edge_code[pl.ds(4 * side, 4), :] = rows_in[side, pl.ds(2 * levels + taps, taps), :]
        edge_weight[pl.ds(4 * side, 4), :] = rows_in[side, pl.ds(2 * levels, taps), :]
    lax.fori_loop(0, length // LANES, block, 0)

    lane = lax.broadcasted_iota(jnp.int32, (8, LANES), 1)
    here = jnp.logical_and(lane >= 2 * levels + taps, lane < 2 * levels + 2 * taps)
    edge_cols = [[], []]
    for side in range(2):
        parts = [[], []]
        for i0 in range(0, height, 8):
            line = cols_in[side, pl.ds(i0, 8), :]
            code = jnp.where(here, line, 0.0).astype(jnp.int32)
            taken = taken_from(
                lambda q, o: sides3[side, q, pl.ds(i0 + 3 * o, 8), :], [code], range(2)
            )
            weight = jnp.where(here, pltpu.roll(line, taps, 1), 0.0)
            for q in range(2):
                parts[q].append(jnp.sum(taken[0][q] * weight, axis=1, keepdims=True))
        for q in range(2):
            edge_cols[side].append(jnp.concatenate(parts[q], axis=0))

    row = lax.broadcasted_iota(jnp.int32, (height, length), 0)
    col = lax.broadcasted_iota(jnp.int32, (height, length), 1)

    def shifted(q, west, east, south, north):
        return (
            jnp.where(row == 0, west, pltpu.roll(q, 1, 0)),
            jnp.where(row == height - 1, east, pltpu.roll(q, height - 1, 0)),
            jnp.where(col == 0, south, pltpu.roll(q, 1, 1)),
            jnp.where(col == length - 1, north, pltpu.roll(q, length - 1, 1)),
        )

    def dx(q, index):
        low = jnp.where(row == 0, edge_rows[index, pl.ds(0, 1), :], pltpu.roll(q, 1, 0))
        high = jnp.where(
            row == height - 1, edge_rows[index, pl.ds(1, 1), :], pltpu.roll(q, height - 1, 0)
        )
        return 0.5 * (high - low)

    def dy(q, index):
        low = jnp.where(col == 0, edge_cols[0][index], pltpu.roll(q, 1, 1))
        high = jnp.where(col == length - 1, edge_cols[1][index], pltpu.roll(q, length - 1, 1))
        return 0.5 * (high - low)

    sxx, sxy, syy = forcing[0], forcing[1], forcing[2]
    force_x = -(dx(sxx, 0) + dy(sxy, 0))
    force_y = -(dx(sxy, 1) + dy(syy, 1))
    wet = sea[...].astype(jnp.float32)
    turn = jnp.broadcast_to(0.5 * coriolis[...], (height, length))
    for level in range(levels):
        decay = math.exp(-level / 3.0)
        here_u, here_v = u[level], v[level]

        def laplace(q, n):
            west, east, south, north = shifted(
                q,
                rows_in[0, pl.ds(n, 1), :],
                rows_in[1, pl.ds(n, 1), :],
                cols_in[0, :, n : n + 1],
                cols_in[1, :, n : n + 1],
            )
            return east + west + north + south - 4.0 * q

        u_out[level] = wet * (
            here_u
            + turn * (here_v + decay * forcing[4])
            + (0.5 * decay) * force_x
            + 0.1 * laplace(here_u, level)
        )
        v_out[level] = wet * (
            here_v
            - turn * (here_u + decay * forcing[3])
            + (0.5 * decay) * force_y
            + 0.1 * laplace(here_v, levels + level)
        )


def local(
    spectrum,
    sea_mask,
    transfer,
    bulk_weight,
    remap_cell,
    remap_weight,
    ocean_u,
    ocean_v,
    ocean_mask,
    coriolis,
):
    f32 = jnp.float32
    components, width, _ = spectrum.shape
    levels, height, length = ocean_u.shape
    taps = remap_cell.shape[2]
    quantities = bulk_weight.shape[0]
    padded = -(-(components + PAIR) // LANES) * LANES
    coef = courant(components, NFREQ)
    cell = jnp.transpose(remap_cell, (0, 2, 1))
    weight = jnp.transpose(remap_weight, (0, 2, 1))
    messages = 2 * levels + 2 * taps
    S = jax.ShapeDtypeStruct
    dma = pltpu.SemaphoreType.DMA
    x1, ghost, cells, weights, rows_in, cols_in = pl.pallas_call(
        wave_kernel,
        name="wave_first",
        out_shape=(
            S((width + 2, components, LANES), f32),
            S((components, LANES), f32),
            S((taps, height, length), jnp.int32),
            S((taps, height, length), f32),
            S((2, messages, length), f32),
            S((2, height, LANES), f32),
        ),
        in_specs=[ANY, VMEM, ANY, ANY, ANY, ANY, ANY, ANY],
        out_specs=(ANY,) * 6,
        scratch_shapes=[
            pltpu.VMEM((width + 4, components, LANES), f32),
            pltpu.VMEM((width + 2, components, LANES), f32),
            pltpu.VMEM((components, (width + 1) * LANES), jnp.bfloat16),
            pltpu.VMEM((components, 2 * LANES), jnp.bfloat16),
            pltpu.VMEM((components, components), jnp.bfloat16),
            pltpu.VMEM((components, 8), f32),
            pltpu.VMEM((width + 4, PAIR, LANES), f32),
            pltpu.VMEM((2, width, LANES), jnp.int32),
            pltpu.VMEM((padded, LANES), f32),
            pltpu.VMEM((32, padded), f32),
            pltpu.VMEM((LANES, padded), f32),
            pltpu.VMEM((padded, LANES), f32),
            pltpu.VMEM((components, LANES), f32),
            pltpu.VMEM((height, taps, length), jnp.int32),
            pltpu.VMEM((height, taps, length), f32),
            pltpu.VMEM((levels, height, length), f32),
            pltpu.VMEM((levels, height, length), f32),
            pltpu.VMEM((taps, height, length), jnp.int32),
            pltpu.VMEM((taps, height, length), f32),
            pltpu.VMEM((2, messages, length), f32),
            pltpu.VMEM((2, height, LANES), f32),
            pltpu.VMEM((2, messages, length), f32),
            pltpu.VMEM((2, height, LANES), f32),
            dma((16,)),
            dma((24,)),
            dma((24,)),
            dma((20,)),
        ],
        compiler_params=pltpu.CompilerParams(
            collective_id=0, has_side_effects=True, vmem_limit_bytes=GRANT
        ),
    )(spectrum, sea_mask, transfer, coef, cell, weight, ocean_u, ocean_v)

    bulk_columns = jnp.pad(bulk_weight.T, ((0, 0), (0, 8 - quantities)))
    spectrum_out, bulk = pl.pallas_call(
        second_kernel,
        name="wave_second",
        out_shape=(S(spectrum.shape, f32), S((quantities, width, LANES), f32)),
        in_specs=[ANY, ANY, VMEM, ANY, ANY, ANY],
        out_specs=(ANY, VMEM),
        scratch_shapes=[
            pltpu.VMEM((width + 2, components, LANES), f32),
            pltpu.VMEM((width, components, LANES), f32),
            pltpu.VMEM((components, width * LANES), jnp.bfloat16),
            pltpu.VMEM((components, components), jnp.bfloat16),
            pltpu.VMEM((components, 8), f32),
            pltpu.VMEM((components, 8), f32),
            pltpu.VMEM((components, LANES), f32),
            dma((24,)),
            dma((24,)),
        ],
        compiler_params=pltpu.CompilerParams(vmem_limit_bytes=GRANT),
    )(x1, ghost, sea_mask, transfer, coef, bulk_columns)

    near, sides, far = pl.pallas_call(
        spread_kernel,
        name="spread",
        out_shape=(
            S((3, quantities, width, LANES), f32),
            S((2, 3, 2, width, LANES), f32),
            S((2, 2, width, LANES), f32),
        ),
        in_specs=[VMEM],
        out_specs=(VMEM,) * 3,
        scratch_shapes=[dma((12,)), dma((12,))],
        compiler_params=pltpu.CompilerParams(collective_id=1, has_side_effects=True),
    )(bulk)

    ocean_u_out, ocean_v_out = pl.pallas_call(
        ocean_kernel,
        name="ocean",
        out_shape=(S(ocean_u.shape, f32), S(ocean_v.shape, f32)),
        in_specs=[VMEM] * 11,
        out_specs=(VMEM, VMEM),
        scratch_shapes=[
            pltpu.VMEM((quantities, 8 + 3 * width + 8, LANES), f32),
            pltpu.VMEM((quantities, 9 * width, LANES), f32),
            pltpu.VMEM((2, 2, 9 * width, LANES), f32),
            pltpu.VMEM((quantities, height, length), f32),
            pltpu.VMEM((8, length), f32),
            pltpu.VMEM((8, length), f32),
            pltpu.VMEM((2, 8, length), f32),
        ],
        compiler_params=pltpu.CompilerParams(vmem_limit_bytes=GRANT),
    )(
        near, sides, far, cells, weights, rows_in, cols_in, ocean_u, ocean_v, ocean_mask,
        coriolis[None],
    )
    return (spectrum_out, ocean_u_out, ocean_v_out)


def solution(mesh):
    placed = (
        P(None, "lon", "lat"),
        P("lon", "lat"),
        P(),
        P(),
        P("lon", "lat", None),
        P("lon", "lat", None),
        P(None, "lon", "lat"),
        P(None, "lon", "lat"),
        P("lon", "lat"),
        P("lat"),
    )
    return jax.shard_map(
        local,
        mesh=mesh,
        in_specs=placed,
        out_specs=(P(None, "lon", "lat"), P(None, "lon", "lat"), P(None, "lon", "lat")),
        check_vma=False,
    )
```

```python
import math

import jax
import jax.numpy as jnp
import numpy as np
from jax import lax
from jax.experimental import pallas as pl
from jax.experimental.pallas import tpu as pltpu
from jax.sharding import PartitionSpec as P

NFREQ = 36
MESH = pl.DeviceIdType.MESH
VMEM = pl.BlockSpec(memory_space=pltpu.VMEM)
ANY = pl.BlockSpec(memory_space=pl.ANY)
LANES = 128
PAIR = 16
GRANT = 60 * 1024 * 1024


def courant(components, freqs):
    index = np.arange(components)
    theta = 2.0 * np.pi * (index // freqs + 0.5) / (components // freqs)
    speed = 1.1 ** -(index % freqs).astype(np.float64)
    east, north = 0.45 * speed * np.cos(theta), 0.45 * speed * np.sin(theta)
    parts = [1.0 - abs(east) - abs(north), abs(east), abs(north)]
    parts += [np.maximum(p, 0.0) for p in (east, -east, north, -north)] + [0.0 * east]
    return np.stack(parts, axis=1).astype(np.float32)


def sign_of(function, first, last, freqs, directions):
    signs = set()
    for d in range(first // freqs, (last - 1) // freqs + 1):
        signs.add(1 if function(2 * math.pi * (d + 0.5) / directions) > 0 else -1)
    return signs.pop() if len(signs) == 1 else 0


def segments(components, freqs):
    directions = components // freqs
    runs = []
    for pair in range(components // PAIR):
        first, last = pair * PAIR, (pair + 1) * PAIR
        key = (
            sign_of(math.cos, first, last, freqs, directions),
            sign_of(math.sin, first, last, freqs, directions),
        )
        if runs and runs[-1][2] == key:
            runs[-1][1] = pair + 1
        else:
            runs.append([pair, pair + 1, key])
    return [(a, b, xs, ys) for a, b, (xs, ys) in runs]


def row_spans(components, freqs, sign):
    spans = []
    for a, b, xs, _ in segments(components, freqs):
        if xs == -sign:
            continue
        if spans and spans[-1][1] == a * PAIR:
            spans[-1][1] = b * PAIR
        else:
            spans.append([a * PAIR, b * PAIR])
    return [tuple(s) for s in spans]


def complement(spans, total):
    out, at = [], 0
    for a, b in spans:
        if a > at:
            out.append((at, a))
        at = b
    if at < total:
        out.append((at, total))
    return out


def south_lane(c):
    return 2 * c + 1 if 0 <= c < 8 else (32 if c < 0 else 33)


def north_lane(c):
    return 16 + 2 * c if 0 <= c < 8 else (34 if c < 0 else 35)


def lane_shift(x, source, target):
    return pltpu.roll(x, (target - source) % LANES, 1)


def coefficients(coef, wide, r, xs, ys):
    rows = pl.ds(r, PAIR)

    def spread(n):
        return jnp.broadcast_to(coef[rows, n : n + 1], (PAIR, LANES))

    return dict(
        c=wide[0, rows, :],
        x=wide[1, rows, :] if xs else (spread(3), spread(4)),
        y=wide[2, rows, :] if ys else (spread(5), spread(6)),
    )


def upwind(co, xs, ys, centre, west, east, south, north):
    result = co["c"] * centre
    if xs:
        result = result + co["x"] * (west() if xs > 0 else east())
    else:
        result = result + co["x"][0] * west() + co["x"][1] * east()
    if ys:
        result = result + co["y"] * (south() if ys > 0 else north())
    else:
        result = result + co["y"][0] * south() + co["y"][1] * north()
    return result


def advect_columns(co, xs, ys, columns, state, ghost, lane):
    out = {}
    for c in columns:
        out[c] = upwind(
            co,
            xs,
            ys,
            state[c],
            lambda: state[c - 1],
            lambda: state[c + 1],
            lambda: jnp.where(
                lane == 0, lane_shift(ghost, south_lane(c), 0), pltpu.roll(state[c], 1, 1)
            ),
            lambda: jnp.where(
                lane == LANES - 1,
                lane_shift(ghost, north_lane(c), LANES - 1),
                pltpu.roll(state[c], LANES - 1, 1),
            ),
        )
    return out


def needed(columns, xs):
    want = set(columns)
    if xs >= 0:
        want |= {c - 1 for c in columns}
    if xs <= 0:
        want |= {c + 1 for c in columns}
    return sorted(want)


def over_rows(runs, body, unroll=10):
    for a, b, xs, ys in runs:
        steps = (b - a) // unroll
        if steps > 1:

            def step(p, carry, a=a, xs=xs, ys=ys):
                for j in range(unroll):
                    body(pl.multiple_of((a + p * unroll + j) * PAIR, PAIR), xs, ys)
                return carry

            lax.fori_loop(0, steps, step, 0)
            a += steps * unroll
        for p in range(a, b):
            body(p * PAIR, xs, ys)


def repeat(count, body, unroll):
    def step(p, carry):
        for j in range(unroll):
            body(p * unroll + j)
        return carry

    lax.fori_loop(0, count // unroll, step, 0)
    for p in range(count // unroll * unroll, count):
        body(p)


def bulk_of(bulk_wide, state, columns, quantities, components, bulk):
    unroll = 9

    def gather(p, totals):
        totals = list(totals)
        for j in range(unroll):
            rows = pl.ds(pl.multiple_of((p * unroll + j) * 8, 8), 8)
            wide = [bulk_wide[q, rows, :] for q in range(quantities)]
            for n, c in enumerate(columns):
                value = state[c + 2, rows, :]
                for q in range(quantities):
                    at = n * quantities + q
                    totals[at] = totals[at] + wide[q] * value
        return tuple(totals)

    zero = jnp.zeros((8, LANES), jnp.float32)
    totals = lax.fori_loop(
        0, components // 8 // unroll, gather, (zero,) * (len(columns) * quantities)
    )
    for n, c in enumerate(columns):
        for q in range(quantities):
            bulk[q, pl.ds(c, 1), :] = jnp.sum(
                totals[n * quantities + q], axis=0, keepdims=True
            )


def wave_kernel(
    spectrum, sea, transfer, coef_hbm, bulk_weight, cell_hbm, weight_hbm, u_hbm, v_hbm,
    s2_out, near_out, sides_out, far_out, cells_out, weights_out, rows_out, cols_out,
    x, a, ab, abe, t, coef, wide, bulk_turned, bulk_wide, masks, packed, turned, gturned, g, ga,
    cell, weight, u, v, cells, weights, rows_send, cols_send, rows_in, cols_in,
    bulk, near, sides, far, far_masks, local_sem, send_sem, recv_sem, out_sem,
):
    lon, lat = lax.axis_index("lon"), lax.axis_index("lat")
    nlon, nlat = lax.axis_size("lon"), lax.axis_size("lat")
    components, width, _ = spectrum.shape
    quantities = bulk_weight.shape[0]
    runs = segments(components, NFREQ)
    plus = row_spans(components, NFREQ, 1)
    minus = row_spans(components, NFREQ, -1)
    around = [lax.rem(lon + d + nlon, nlon) for d in (-2, -1, 0, 1, 2)]
    east, west = around[3], around[1]
    has_south, has_north = lat > 0, lat < nlat - 1
    lane = lax.broadcasted_iota(jnp.int32, (PAIR, LANES), 1)

    gturned[...] = jnp.zeros_like(gturned)
    cols_in[...] = jnp.zeros_like(cols_in)
    sides[...] = jnp.zeros_like(sides)

    local = []

    def load(src, dst):
        copy = pltpu.make_async_copy(src, dst, local_sem.at[len(local)])
        copy.start()
        local.append(copy)
        return copy

    barrier = pltpu.get_barrier_semaphore()

    def greet(to_lon, to_lat):
        pl.semaphore_signal(barrier, inc=1, device_id=(to_lon, to_lat), device_id_type=MESH)

    for d in (0, 1, 3, 4):
        greet(around[d], lat)

    @pl.when(has_north)
    def _():
        for d in (1, 2, 3):
            greet(around[d], lat + 1)

    @pl.when(has_south)
    def _():
        for d in (1, 2, 3):
            greet(around[d], lat - 1)

    columns_in = [load(spectrum.at[:, c, :], x.at[c + 2]) for c in range(width)]
    coef_in = load(coef_hbm, coef)
    cell_in = load(cell_hbm, cell)
    weight_in = load(weight_hbm, weight)
    u_in = load(u_hbm, u)
    v_in = load(v_hbm, v)
    transfer_in = load(transfer, t)

    pl.semaphore_wait(
        barrier, 4 + 3 * has_north.astype(jnp.int32) + 3 * has_south.astype(jnp.int32)
    )

    count = [0]

    def remote(src, dst, to_lon, to_lat):
        n = count[0]
        count[0] += 1
        return pltpu.make_async_remote_copy(
            src_ref=src,
            dst_ref=dst,
            send_sem=send_sem.at[n],
            recv_sem=recv_sem.at[n],
            device_id=(to_lon, to_lat),
            device_id_type=MESH,
        )

    def columns(spans, source, target, to_lon):
        return [
            remote(source(pl.ds(k0, k1 - k0)), target(pl.ds(k0, k1 - k0)), to_lon, lat)
            for k0, k1 in spans
        ]

    first = columns(
        plus, lambda k: spectrum.at[k, width - 1, :], lambda k: x.at[1, k, :], east
    ) + columns(minus, lambda k: spectrum.at[k, 0, :], lambda k: x.at[width + 2, k, :], west)
    second = columns(
        plus, lambda k: a.at[width, k, :], lambda k: a.at[0, k, :], east
    ) + columns(minus, lambda k: a.at[1, k, :], lambda k: a.at[width + 1, k, :], west)
    side_masks = [
        remote(sea.at[pl.ds(width - 1, 1), :], far_masks.at[0], east, lat),
        remote(sea.at[pl.ds(0, 1), :], far_masks.at[1], west, lat),
    ]
    for copy in side_masks + first:
        copy.start()

    for c in range(width):
        masks[c + 2] = jnp.broadcast_to(
            sea[pl.ds(c, 1), :].astype(jnp.float32), (PAIR, LANES)
        )

    for copy in columns_in:
        copy.wait()

    def pack(r, values):
        total = jnp.zeros((PAIR, LANES), jnp.float32)
        half = lane // 2
        for c in range(width):
            total = jnp.where(half == c, lane_shift(values[c], LANES - 2, 2 * c), total)
            total = jnp.where(half == 8 + c, lane_shift(values[c], 0, 16 + 2 * c), total)
        packed[pl.ds(r, PAIR), :] = total

    def pack_rows(p):
        r = pl.multiple_of(p * PAIR, PAIR)
        values = []
        for c in range(width):
            value = x[c + 2, pl.ds(r, PAIR), :] * masks[c + 2]
            x[c + 2, pl.ds(r, PAIR), :] = value
            values.append(value)
        pack(r, values)

    repeat(components // PAIR, pack_rows, 9)
    pack(components, [masks[c + 2] for c in range(width)])
    blocks = packed.shape[0] // LANES
    tail = components + PAIR
    packed[pl.ds(tail, blocks * LANES - tail), :] = jnp.zeros(
        (blocks * LANES - tail, LANES), jnp.float32
    )
    for b in range(blocks):
        turned[:, b * LANES : (b + 1) * LANES] = jnp.transpose(
            packed[b * LANES : (b + 1) * LANES, :]
        )[:32, :]

    to_north = [
        remote(turned.at[pl.ds(0, 16), :], gturned.at[pl.ds(0, 16), :], lon, lat + 1),
        remote(turned.at[pl.ds(15, 1), :], gturned.at[pl.ds(32, 1), :], east, lat + 1),
        remote(turned.at[pl.ds(1, 1), :], gturned.at[pl.ds(33, 1), :], west, lat + 1),
    ]
    to_south = [
        remote(turned.at[pl.ds(16, 16), :], gturned.at[pl.ds(16, 16), :], lon, lat - 1),
        remote(turned.at[pl.ds(30, 1), :], gturned.at[pl.ds(34, 1), :], east, lat - 1),
        remote(turned.at[pl.ds(16, 1), :], gturned.at[pl.ds(35, 1), :], west, lat - 1),
    ]

    @pl.when(has_north)
    def _():
        for copy in to_north:
            copy.start()

    @pl.when(has_south)
    def _():
        for copy in to_south:
            copy.start()

    coef_in.wait()
    bulk_turned[...] = jnp.zeros_like(bulk_turned)
    for b in range(blocks):
        low = b * LANES
        high = min(low + LANES, components)
        bulk_turned[pl.ds(0, quantities), : high - low] = bulk_weight[:, low:high]
        part = jnp.transpose(bulk_turned[...])
        rows = pl.ds(low, high - low)
        for q in range(quantities):
            bulk_wide[q, rows, :] = jnp.broadcast_to(
                part[: high - low, q : q + 1], (high - low, LANES)
            )

    def widen(p):
        rows = pl.ds(pl.multiple_of(p * PAIR, PAIR), PAIR)
        line = coef[rows, :]
        for n in range(3):
            wide[n, rows, :] = jnp.broadcast_to(line[:, n : n + 1], (PAIR, LANES))

    repeat(components // PAIR, widen, 9)

    for copy in (cell_in, weight_in, u_in, v_in):
        copy.wait()
    height, taps, length = cell.shape
    for i in range(height):
        for tap in range(taps):
            cells[tap, pl.ds(i, 1), :] = cell[i, pl.ds(tap, 1), :]
            weights[tap, pl.ds(i, 1), :] = weight[i, pl.ds(tap, 1), :]
    levels = u.shape[0]
    for side, row in ((0, height - 1), (1, 0)):
        for level in range(levels):
            rows_send[side, pl.ds(level, 1), :] = u[level, pl.ds(row, 1), :]
            rows_send[side, pl.ds(levels + level, 1), :] = v[level, pl.ds(row, 1), :]
        for tap in range(taps):
            rows_send[side, pl.ds(2 * levels + tap, 1), :] = weights[tap, pl.ds(row, 1), :]
            rows_send[side, pl.ds(2 * levels + taps + tap, 1), :] = cells[
                tap, pl.ds(row, 1), :
            ].astype(jnp.float32)
    lane_all = lax.broadcasted_iota(jnp.int32, (height, LANES), 1)
    for side, start, source in ((0, length - LANES, LANES - 1), (1, 0, 0)):
        total = jnp.zeros((height, LANES), jnp.float32)
        for n in range(2 * levels + 2 * taps):
            if n < levels:
                block = u[n, :, start : start + LANES]
            elif n < 2 * levels:
                block = v[n - levels, :, start : start + LANES]
            elif n < 2 * levels + taps:
                block = weights[n - 2 * levels, :, start : start + LANES]
            else:
                block = cells[n - 2 * levels - taps, :, start : start + LANES].astype(jnp.float32)
            total = jnp.where(lane_all == n, lane_shift(block, source, n), total)
        cols_send[side] = total

    stores = []

    def store(src, dst):
        copy = pltpu.make_async_copy(src, dst, out_sem.at[len(stores)])
        copy.start()
        stores.append(copy)

    store(cells, cells_out)
    store(weights, weights_out)

    @pl.when(has_south)
    def _():
        for copy in to_north:
            copy.wait_recv()

    @pl.when(has_north)
    def _():
        for copy in to_south:
            copy.wait_recv()

    for b in range(blocks):
        g[b * LANES : (b + 1) * LANES, :] = jnp.transpose(
            gturned[:, b * LANES : (b + 1) * LANES]
        )
    inner = list(range(1, width - 1))
    outer = [0, width - 1]
    ghost_at = len(inner) * LANES

    def first_inner(r, xs, ys):
        co = coefficients(coef, wide, r, xs, ys)
        rows = pl.ds(r, PAIR)
        state = {c: x[c + 2, rows, :] for c in needed(inner, xs)}
        ghost = g[rows, :]
        mine = packed[rows, :]
        for c, value in advect_columns(co, xs, ys, inner, state, ghost, lane).items():
            a[c + 1, rows, :] = value
            ab[rows, (c - 1) * LANES : c * LANES] = value.astype(jnp.bfloat16)

        def sideways(step, low, high):
            moved = pltpu.roll(ghost, step % LANES, 1)
            for target, source in (low, high):
                moved = jnp.where(lane == target, lane_shift(ghost, source, target), moved)
            return moved

        value = upwind(
            co,
            xs,
            ys,
            ghost,
            lambda: sideways(2, (1, 32), (16, 34)),
            lambda: sideways(-2, (15, 33), (30, 35)),
            lambda: jnp.where(lane < 16, pltpu.roll(ghost, 1, 1), pltpu.roll(mine, 15, 1)),
            lambda: jnp.where(
                lane < 16, pltpu.roll(mine, LANES - 15, 1), pltpu.roll(ghost, LANES - 1, 1)
            ),
        )
        ga[rows, :] = value
        ab[rows, ghost_at : ghost_at + LANES] = value.astype(jnp.bfloat16)

    over_rows(runs, first_inner)
    transfer_in.wait()
    block = 432
    ghost_mask = g[pl.ds(components, 1), :]

    def inner_product(state, shift, with_ghost):
        def product(m, carry):
            rows = pl.ds(pl.multiple_of(m * block, PAIR), block)
            for n in range(0, len(inner), 2):
                added = jnp.dot(
                    t[rows, :],
                    ab[:, n * LANES : (n + 2) * LANES],
                    preferred_element_type=jnp.float32,
                )
                for c in (n + 1, n + 2):
                    part = added[:, (c - n - 1) * LANES : (c - n) * LANES]
                    state[c + shift, rows, :] = masks[c + 2, pl.ds(0, 1), :] * (
                        state[c + shift, rows, :] + 0.5 * part
                    )
            if with_ghost:
                added = jnp.dot(
                    t[rows, :],
                    ab[:, ghost_at : ghost_at + LANES],
                    preferred_element_type=jnp.float32,
                )
                ga[rows, :] = ghost_mask * (ga[rows, :] + 0.5 * added)
            return carry

        lax.fori_loop(0, components // block, product, 0)

    def outer_product(state, shift):
        def product(m, carry):
            rows = pl.ds(pl.multiple_of(m * block, PAIR), block)
            added = jnp.dot(t[rows, :], abe[...], preferred_element_type=jnp.float32)
            for n, c in enumerate(outer):
                part = added[:, n * LANES : (n + 1) * LANES]
                state[c + shift, rows, :] = masks[c + 2, pl.ds(0, 1), :] * (
                    state[c + shift, rows, :] + 0.5 * part
                )
            return carry

        lax.fori_loop(0, components // block, product, 0)

    inner_product(a, 1, True)

    for copy in side_masks + first:
        copy.wait_recv()
    rows_copy = [
        remote(rows_send.at[0], rows_in.at[0], east, lat),
        remote(rows_send.at[1], rows_in.at[1], west, lat),
    ]
    cols_north = remote(cols_send.at[0], cols_in.at[0], lon, lat + 1)
    cols_south = remote(cols_send.at[1], cols_in.at[1], lon, lat - 1)
    for copy in rows_copy:
        copy.start()

    @pl.when(has_north)
    def _():
        cols_north.start()

    @pl.when(has_south)
    def _():
        cols_south.start()

    for slot, side in ((1, 0), (width + 2, 1)):
        masks[slot] = jnp.broadcast_to(far_masks[side].astype(jnp.float32), (PAIR, LANES))

    def first_outer(r, xs, ys):
        co = coefficients(coef, wide, r, xs, ys)
        rows = pl.ds(r, PAIR)
        state = {}
        for c in needed(outer, xs):
            value = x[c + 2, rows, :]
            state[c] = value * masks[c + 2] if c in (-1, width) else value
        for n, (c, value) in enumerate(
            advect_columns(co, xs, ys, outer, state, g[rows, :], lane).items()
        ):
            a[c + 1, rows, :] = value
            abe[rows, n * LANES : (n + 1) * LANES] = value.astype(jnp.bfloat16)

    over_rows(runs, first_outer)
    outer_product(a, 1)
    for copy in second:
        copy.start()

    def second_step(group, target):
        def step(r, xs, ys):
            co = coefficients(coef, wide, r, xs, ys)
            rows = pl.ds(r, PAIR)
            state = {c: a[c + 1, rows, :] for c in needed(group, xs)}
            for n, (c, value) in enumerate(
                advect_columns(co, xs, ys, group, state, ga[rows, :], lane).items()
            ):
                x[c + 2, rows, :] = value
                target[rows, n * LANES : (n + 1) * LANES] = value.astype(jnp.bfloat16)

        over_rows(runs, step)

    for copy in side_masks + first:
        copy.wait_send()
    second_step(inner, ab)
    inner_product(x, 2, False)
    for c in inner:
        store(x.at[c + 2], s2_out.at[c])
    bulk_of(bulk_wide, x, inner, quantities, components, bulk)

    for copy in second:
        copy.wait_recv()
    second_step(outer, abe)
    outer_product(x, 2)
    for c in outer:
        store(x.at[c + 2], s2_out.at[c])
    bulk_of(bulk_wide, x, outer, quantities, components, bulk)

    drift = bulk.at[pl.ds(1, 2)]
    stress = bulk.at[pl.ds(0, 2)]
    flat = [
        remote(bulk, near.at[2], west, lat),
        remote(bulk, near.at[0], east, lat),
        remote(stress, far.at[1], around[0], lat),
        remote(stress, far.at[0], around[4], lat),
    ]
    spread_north = [
        remote(drift, sides.at[0, 2], west, lat + 1),
        remote(drift, sides.at[0, 1], lon, lat + 1),
        remote(drift, sides.at[0, 0], east, lat + 1),
    ]
    spread_south = [
        remote(drift, sides.at[1, 2], west, lat - 1),
        remote(drift, sides.at[1, 1], lon, lat - 1),
        remote(drift, sides.at[1, 0], east, lat - 1),
    ]
    for copy in flat:
        copy.start()

    @pl.when(has_north)
    def _():
        for copy in spread_north:
            copy.start()

    @pl.when(has_south)
    def _():
        for copy in spread_south:
            copy.start()

    near[1] = bulk[...]

    for copy in rows_copy:
        copy.wait()
    for copy in second:
        copy.wait_send()

    @pl.when(has_north)
    def _():
        for copy in to_north + [cols_north]:
            copy.wait_send()
        cols_south.wait_recv()

    @pl.when(has_south)
    def _():
        for copy in to_south + [cols_south]:
            copy.wait_send()
        cols_north.wait_recv()

    store(rows_in, rows_out)
    store(cols_in, cols_out)

    for copy in flat:
        copy.wait()

    @pl.when(has_north)
    def _():
        for copy in spread_north:
            copy.wait_send()
        for copy in spread_south:
            copy.wait_recv()

    @pl.when(has_south)
    def _():
        for copy in spread_south:
            copy.wait_send()
        for copy in spread_north:
            copy.wait_recv()

    store(near, near_out)
    store(sides, sides_out)
    store(far, far_out)
    for copy in stores:
        copy.wait()


def taken_from(sources, codes, quantities):
    places = [c & (LANES - 1) for c in codes]
    offsets = [c >> 9 for c in codes]
    taken = [[jnp.zeros(codes[0].shape, jnp.float32)] * len(quantities) for _ in codes]
    for o in range(17):
        hits = [offset == o for offset in offsets]
        for n, q in enumerate(quantities):
            source = sources(q, o)
            for i in range(len(codes)):
                got = jnp.take_along_axis(source, places[i], axis=1, mode="promise_in_bounds")
                taken[i][n] = jnp.where(hits[i], got, taken[i][n])
    return taken


def ocean_kernel(
    s2, near, sides, far, cells, weights, rows_in, cols_in, u, v, sea, coriolis,
    spectrum_out, u_out, v_out,
    near1, near3, sides3, forcing, edge_code, edge_weight, edge_rows, state, in_sem, out_sem,
):
    quantities = near.shape[1]
    width = near.shape[2]
    taps, height, length = cells.shape
    levels = u.shape[0]
    reads = [pltpu.make_async_copy(s2.at[c], state.at[c], in_sem.at[c]) for c in range(width)]
    writes = [
        pltpu.make_async_copy(state.at[c], spectrum_out.at[:, c, :], out_sem.at[c])
        for c in range(width)
    ]
    for copy in reads:
        copy.start()
    for part in range(3):
        near1[:, pl.ds(8 + part * width, width), :] = near[part]
    near1[pl.ds(0, 2), pl.ds(7, 1), :] = far[0, :, pl.ds(width - 1, 1), :]
    near1[pl.ds(0, 2), pl.ds(8 + 3 * width, 1), :] = far[1, :, pl.ds(0, 1), :]
    for i in range(3 * width):
        for q in range(quantities):
            near3[q, pl.ds(3 * i, 3), :] = jnp.broadcast_to(
                near1[q, pl.ds(8 + i, 1), :], (3, LANES)
            )
        for side in range(2):
            for q in range(2):
                sides3[side, q, pl.ds(3 * i, 3), :] = jnp.broadcast_to(
                    sides[side, i // width, q, pl.ds(i % width, 1), :], (3, LANES)
                )

    def block(jb, carry):
        lanes = pl.ds(pl.multiple_of(jb * LANES, LANES), LANES)
        for i0 in range(0, height, 8):
            rows = pl.ds(i0, 8)
            taken = taken_from(
                lambda q, o: near3[q, pl.ds(i0 + 3 * o, 8), :],
                [cells[tap, rows, lanes] for tap in range(taps)],
                range(quantities),
            )
            for q in range(quantities):
                total = 0.0
                for tap in range(taps):
                    total = total + taken[tap][q] * weights[tap, rows, lanes]
                forcing[q, rows, lanes] = total
        low = lax.broadcasted_iota(jnp.int32, (8, LANES), 0) < 4
        taken = taken_from(
            lambda q, o: jnp.where(
                low,
                jnp.broadcast_to(near1[q, pl.ds(7 + o, 1), :], (8, LANES)),
                jnp.broadcast_to(near1[q, pl.ds(16 + o, 1), :], (8, LANES)),
            ),
            [edge_code[:, lanes].astype(jnp.int32)],
            range(2),
        )
        for q in range(2):
            product = taken[0][q] * edge_weight[:, lanes]
            zero = jnp.zeros_like(product)
            edge_rows[q, pl.ds(0, 1), lanes] = jnp.sum(
                jnp.where(low, product, zero), axis=0, keepdims=True
            )
            edge_rows[q, pl.ds(1, 1), lanes] = jnp.sum(
                jnp.where(low, zero, product), axis=0, keepdims=True
            )
        return carry

    for read, write in zip(reads, writes):
        read.wait()
        write.start()
    for side in range(2):
        edge_code[pl.ds(4 * side, 4), :] = rows_in[side, pl.ds(2 * levels + taps, taps), :]
        edge_weight[pl.ds(4 * side, 4), :] = rows_in[side, pl.ds(2 * levels, taps), :]
    lax.fori_loop(0, length // LANES, block, 0)

    lane = lax.broadcasted_iota(jnp.int32, (8, LANES), 1)
    here = jnp.logical_and(lane >= 2 * levels + taps, lane < 2 * levels + 2 * taps)
    edge_cols = [[], []]
    for side in range(2):
        parts = [[], []]
        for i0 in range(0, height, 8):
            line = cols_in[side, pl.ds(i0, 8), :]
            code = jnp.where(here, line, 0.0).astype(jnp.int32)
            taken = taken_from(
                lambda q, o: sides3[side, q, pl.ds(i0 + 3 * o, 8), :], [code], range(2)
            )
            weight = jnp.where(here, pltpu.roll(line, taps, 1), 0.0)
            for q in range(2):
                parts[q].append(jnp.sum(taken[0][q] * weight, axis=1, keepdims=True))
        for q in range(2):
            edge_cols[side].append(jnp.concatenate(parts[q], axis=0))

    row = lax.broadcasted_iota(jnp.int32, (height, length), 0)
    col = lax.broadcasted_iota(jnp.int32, (height, length), 1)

    def shifted(q, west, east, south, north):
        return (
            jnp.where(row == 0, west, pltpu.roll(q, 1, 0)),
            jnp.where(row == height - 1, east, pltpu.roll(q, height - 1, 0)),
            jnp.where(col == 0, south, pltpu.roll(q, 1, 1)),
            jnp.where(col == length - 1, north, pltpu.roll(q, length - 1, 1)),
        )

    def dx(q, index):
        low = jnp.where(row == 0, edge_rows[index, pl.ds(0, 1), :], pltpu.roll(q, 1, 0))
        high = jnp.where(
            row == height - 1, edge_rows[index, pl.ds(1, 1), :], pltpu.roll(q, height - 1, 0)
        )
        return 0.5 * (high - low)

    def dy(q, index):
        low = jnp.where(col == 0, edge_cols[0][index], pltpu.roll(q, 1, 1))
        high = jnp.where(col == length - 1, edge_cols[1][index], pltpu.roll(q, length - 1, 1))
        return 0.5 * (high - low)

    sxx, sxy, syy = forcing[0], forcing[1], forcing[2]
    force_x = -(dx(sxx, 0) + dy(sxy, 0))
    force_y = -(dx(sxy, 1) + dy(syy, 1))
    wet = sea[...].astype(jnp.float32)
    turn = jnp.broadcast_to(0.5 * coriolis[...][None], (height, length))
    for level in range(levels):
        decay = math.exp(-level / 3.0)
        here_u, here_v = u[level], v[level]

        def laplace(q, n):
            west, east, south, north = shifted(
                q,
                rows_in[0, pl.ds(n, 1), :],
                rows_in[1, pl.ds(n, 1), :],
                cols_in[0, :, n : n + 1],
                cols_in[1, :, n : n + 1],
            )
            return east + west + north + south - 4.0 * q

        u_out[level] = wet * (
            here_u
            + turn * (here_v + decay * forcing[4])
            + (0.5 * decay) * force_x
            + 0.1 * laplace(here_u, level)
        )
        v_out[level] = wet * (
            here_v
            - turn * (here_u + decay * forcing[3])
            + (0.5 * decay) * force_y
            + 0.1 * laplace(here_v, levels + level)
        )
    for copy in writes:
        copy.wait()


def local(
    spectrum,
    sea_mask,
    transfer,
    bulk_weight,
    remap_cell,
    remap_weight,
    ocean_u,
    ocean_v,
    ocean_mask,
    coriolis,
):
    f32, i32 = jnp.float32, jnp.int32
    components, width, _ = spectrum.shape
    levels, height, length = ocean_u.shape
    taps = remap_cell.shape[2]
    quantities = bulk_weight.shape[0]
    padded = -(-(components + PAIR) // LANES) * LANES
    coef = courant(components, NFREQ)
    cell = jnp.transpose(remap_cell, (0, 2, 1))
    weight = jnp.transpose(remap_weight, (0, 2, 1))
    messages = 2 * levels + 2 * taps
    S = jax.ShapeDtypeStruct
    dma = pltpu.SemaphoreType.DMA
    near_shape = (3, quantities, width, LANES)
    sides_shape = (2, 3, 2, width, LANES)
    far_shape = (2, 2, width, LANES)
    s2, near, sides, far, cells, weights, rows_in, cols_in = pl.pallas_call(
        wave_kernel,
        name="wave",
        out_shape=(
            S((width, components, LANES), f32),
            S(near_shape, f32),
            S(sides_shape, f32),
            S(far_shape, f32),
            S((taps, height, length), i32),
            S((taps, height, length), f32),
            S((2, messages, length), f32),
            S((2, height, LANES), f32),
        ),
        in_specs=[ANY, VMEM, ANY, ANY, VMEM, ANY, ANY, ANY, ANY],
        out_specs=(ANY,) * 8,
        scratch_shapes=[
            pltpu.VMEM((width + 4, components, LANES), f32),
            pltpu.VMEM((width + 2, components, LANES), f32),
            pltpu.VMEM((components, (width - 1) * LANES), jnp.bfloat16),
            pltpu.VMEM((components, 2 * LANES), jnp.bfloat16),
            pltpu.VMEM((components, components), jnp.bfloat16),
            pltpu.VMEM((components, 8), f32),
            pltpu.VMEM((3, components, LANES), f32),
            pltpu.VMEM((LANES, LANES), f32),
            pltpu.VMEM((quantities, components, LANES), f32),
            pltpu.VMEM((width + 4, PAIR, LANES), f32),
            pltpu.VMEM((padded, LANES), f32),
            pltpu.VMEM((32, padded), f32),
            pltpu.VMEM((LANES, padded), f32),
            pltpu.VMEM((padded, LANES), f32),
            pltpu.VMEM((components, LANES), f32),
            pltpu.VMEM((height, taps, length), i32),
            pltpu.VMEM((height, taps, length), f32),
            pltpu.VMEM((levels, height, length), f32),
            pltpu.VMEM((levels, height, length), f32),
            pltpu.VMEM((taps, height, length), i32),
            pltpu.VMEM((taps, height, length), f32),
            pltpu.VMEM((2, messages, length), f32),
            pltpu.VMEM((2, height, LANES), f32),
            pltpu.VMEM((2, messages, length), f32),
            pltpu.VMEM((2, height, LANES), f32),
            pltpu.VMEM((quantities, width, LANES), f32),
            pltpu.VMEM(near_shape, f32),
            pltpu.VMEM(sides_shape, f32),
            pltpu.VMEM(far_shape, f32),
            pltpu.VMEM((2, 1, LANES), i32),
            dma((16,)),
            dma((32,)),
            dma((32,)),
            dma((16,)),
        ],
        compiler_params=pltpu.CompilerParams(
            collective_id=0, has_side_effects=True, vmem_limit_bytes=GRANT
        ),
    )(
        spectrum, sea_mask, transfer, jnp.asarray(coef), bulk_weight, cell, weight,
        ocean_u, ocean_v,
    )

    return pl.pallas_call(
        ocean_kernel,
        name="ocean",
        out_shape=(S(spectrum.shape, f32), S(ocean_u.shape, f32), S(ocean_v.shape, f32)),
        in_specs=[ANY] + [VMEM] * 11,
        out_specs=(ANY, VMEM, VMEM),
        scratch_shapes=[
            pltpu.VMEM((quantities, 8 + 3 * width + 8, LANES), f32),
            pltpu.VMEM((quantities, 9 * width, LANES), f32),
            pltpu.VMEM((2, 2, 9 * width, LANES), f32),
            pltpu.VMEM((quantities, height, length), f32),
            pltpu.VMEM((8, length), f32),
            pltpu.VMEM((8, length), f32),
            pltpu.VMEM((2, 8, length), f32),
            pltpu.VMEM((width, components, LANES), f32),
            dma((width,)),
            dma((width,)),
        ],
        compiler_params=pltpu.CompilerParams(vmem_limit_bytes=GRANT),
    )(
        s2, near, sides, far, cells, weights, rows_in, cols_in, ocean_u, ocean_v, ocean_mask,
        coriolis,
    )


def solution(mesh):
    placed = (
        P(None, "lon", "lat"),
        P("lon", "lat"),
        P(),
        P(),
        P("lon", "lat", None),
        P("lon", "lat", None),
        P(None, "lon", "lat"),
        P(None, "lon", "lat"),
        P("lon", "lat"),
        P("lat"),
    )
    return jax.shard_map(
        local,
        mesh=mesh,
        in_specs=placed,
        out_specs=(P(None, "lon", "lat"), P(None, "lon", "lat"), P(None, "lon", "lat")),
        check_vma=False,
    )
```

```python
import math

import jax
import jax.numpy as jnp
import numpy as np
from jax import lax
from jax.experimental import pallas as pl
from jax.experimental.pallas import tpu as pltpu
from jax.sharding import PartitionSpec as P

NFREQ = 36
MESH = pl.DeviceIdType.MESH
VMEM = pl.BlockSpec(memory_space=pltpu.VMEM)
ANY = pl.BlockSpec(memory_space=pl.ANY)
HBM = pl.BlockSpec(memory_space=pltpu.HBM)
LANES = 128
PAIR = 16
OCEAN_GRANT = 12000 * 1024
WAVE_GRANT = 40000 * 1024
HEAD = 176


def courant(components, freqs):
    index = np.arange(components)
    theta = 2.0 * np.pi * (index // freqs + 0.5) / (components // freqs)
    speed = 1.1 ** -(index % freqs).astype(np.float64)
    east, north = 0.45 * speed * np.cos(theta), 0.45 * speed * np.sin(theta)
    parts = [1.0 - abs(east) - abs(north), abs(east), abs(north)]
    parts += [np.maximum(p, 0.0) for p in (east, -east, north, -north)] + [0.0 * east]
    return np.stack(parts, axis=1).astype(np.float32)


def sign_of(function, first, last, freqs, directions):
    signs = set()
    for d in range(first // freqs, (last - 1) // freqs + 1):
        signs.add(1 if function(2 * math.pi * (d + 0.5) / directions) > 0 else -1)
    return signs.pop() if len(signs) == 1 else 0


def in_hbm(value):
    return pltpu.with_memory_space_constraint(value, pltpu.HBM)


def segments(components, freqs):
    directions = components // freqs
    runs = []
    for pair in range(components // PAIR):
        first, last = pair * PAIR, (pair + 1) * PAIR
        key = (
            sign_of(math.cos, first, last, freqs, directions),
            sign_of(math.sin, first, last, freqs, directions),
        )
        if runs and runs[-1][2] == key:
            runs[-1][1] = pair + 1
        else:
            runs.append([pair, pair + 1, key])
    return [(a, b, xs, ys) for a, b, (xs, ys) in runs]


def row_spans(components, freqs, sign):
    spans = []
    for a, b, xs, _ in segments(components, freqs):
        if xs == -sign:
            continue
        if spans and spans[-1][1] == a * PAIR:
            spans[-1][1] = b * PAIR
        else:
            spans.append([a * PAIR, b * PAIR])
    return [tuple(s) for s in spans]


def split(spans, rows):
    a, b = spans[0]
    return [(a, a + rows)], [(a + rows, b)] + list(spans[1:])


def south_lane(c):
    return 2 * c + 1 if 0 <= c < 8 else (32 if c < 0 else 33)


def north_lane(c):
    return 16 + 2 * c if 0 <= c < 8 else (34 if c < 0 else 35)


def lane_shift(x, source, target):
    return pltpu.roll(x, (target - source) % LANES, 1)


def lanes_of(x, index):
    return jnp.take_along_axis(x, index, axis=1, mode="promise_in_bounds")


def coefficients(coef, wide, r, xs, ys):
    rows = pl.ds(r, PAIR)

    def spread(n):
        return jnp.broadcast_to(coef[rows, n : n + 1], (PAIR, LANES))

    return dict(
        c=wide[0, rows, :],
        x=wide[1, rows, :] if xs else (spread(3), spread(4)),
        y=wide[2, rows, :] if ys else (spread(5), spread(6)),
    )


def upwind(co, xs, ys, centre, west, east, south, north):
    result = co["c"] * centre
    if xs:
        result = result + co["x"] * (west() if xs > 0 else east())
    else:
        result = result + co["x"][0] * west() + co["x"][1] * east()
    if ys:
        result = result + co["y"] * (south() if ys > 0 else north())
    else:
        result = result + co["y"][0] * south() + co["y"][1] * north()
    return result


def advect_columns(co, xs, ys, columns, state, ghost, lane):
    out = {}
    for c in columns:
        out[c] = upwind(
            co,
            xs,
            ys,
            state[c],
            lambda: state[c - 1],
            lambda: state[c + 1],
            lambda: jnp.where(
                lane == 0, lane_shift(ghost, south_lane(c), 0), pltpu.roll(state[c], 1, 1)
            ),
            lambda: jnp.where(
                lane == LANES - 1,
                lane_shift(ghost, north_lane(c), LANES - 1),
                pltpu.roll(state[c], LANES - 1, 1),
            ),
        )
    return out


def needed(columns, xs):
    want = set(columns)
    if xs >= 0:
        want |= {c - 1 for c in columns}
    if xs <= 0:
        want |= {c + 1 for c in columns}
    return sorted(want)


def over_rows(runs, body, unroll=10):
    for a, b, xs, ys in runs:
        steps = (b - a) // unroll
        if steps > 1:

            def step(p, carry, a=a, xs=xs, ys=ys):
                for j in range(unroll):
                    body(pl.multiple_of((a + p * unroll + j) * PAIR, PAIR), xs, ys)
                return carry

            lax.fori_loop(0, steps, step, 0)
            a += steps * unroll
        for p in range(a, b):
            body(p * PAIR, xs, ys)


def repeat(count, body, unroll):
    def step(p, carry):
        for j in range(unroll):
            body(p * unroll + j)
        return carry

    lax.fori_loop(0, count // unroll, step, 0)
    for p in range(count // unroll * unroll, count):
        body(p)


def bulk_of(bulk_wide, state, columns, quantities, components, bulk):
    unroll = 9

    def gather(p, totals):
        totals = list(totals)
        for j in range(unroll):
            rows = pl.ds(pl.multiple_of((p * unroll + j) * 8, 8), 8)
            wide = [bulk_wide[q, rows, :] for q in range(quantities)]
            for n, c in enumerate(columns):
                value = state[c + 2, rows, :]
                for q in range(quantities):
                    at = n * quantities + q
                    totals[at] = totals[at] + wide[q] * value
        return tuple(totals)

    zero = jnp.zeros((8, LANES), jnp.float32)
    totals = lax.fori_loop(
        0, components // 8 // unroll, gather, (zero,) * (len(columns) * quantities)
    )
    for n, c in enumerate(columns):
        for q in range(quantities):
            bulk[q, pl.ds(c, 1), :] = jnp.sum(
                totals[n * quantities + q], axis=0, keepdims=True
            )


def wave_kernel(
    spectrum, sea, transfer, coef_hbm, bulk_weight, cell_hbm, weight_hbm, u_hbm, v_hbm,
    s2_out, near_out, sides_out, far_out, cells_out, weights_out, rows_out, cols_out,
    x, a, ab, abe, t, coef, wide, bulk_turned, bulk_wide, masks, packed, turned, gturned, g, ga,
    cell, weight, u, v, cells, weights, rows_send, cols_send, rows_in, cols_in,
    bulk, near, sides, far, far_masks, local_sem, send_sem, recv_sem, out_sem,
):
    lon, lat = lax.axis_index("lon"), lax.axis_index("lat")
    nlon, nlat = lax.axis_size("lon"), lax.axis_size("lat")
    components, width, _ = spectrum.shape
    quantities = bulk_weight.shape[0]
    runs = segments(components, NFREQ)
    plus = row_spans(components, NFREQ, 1)
    minus = row_spans(components, NFREQ, -1)
    around = [lax.rem(lon + d + nlon, nlon) for d in (-2, -1, 0, 1, 2)]
    east, west = around[3], around[1]
    has_south, has_north = lat > 0, lat < nlat - 1
    lane = lax.broadcasted_iota(jnp.int32, (PAIR, LANES), 1)

    gturned[...] = jnp.zeros_like(gturned)
    cols_in[...] = jnp.zeros_like(cols_in)
    sides[...] = jnp.zeros_like(sides)

    local = []

    def load(src, dst):
        copy = pltpu.make_async_copy(src, dst, local_sem.at[len(local)])
        copy.start()
        local.append(copy)
        return copy

    barrier = pltpu.get_barrier_semaphore()

    def greet(to_lon, to_lat):
        pl.semaphore_signal(barrier, inc=1, device_id=(to_lon, to_lat), device_id_type=MESH)

    for d in (0, 1, 3, 4):
        greet(around[d], lat)

    @pl.when(has_north)
    def _():
        for d in (1, 2, 3):
            greet(around[d], lat + 1)

    @pl.when(has_south)
    def _():
        for d in (1, 2, 3):
            greet(around[d], lat - 1)

    columns_in = [load(spectrum.at[:, c, :], x.at[c + 2]) for c in range(width)]
    coef_in = load(coef_hbm, coef)
    cell_in = load(cell_hbm, cell)
    weight_in = load(weight_hbm, weight)
    u_in = load(u_hbm, u)
    v_in = load(v_hbm, v)
    transfer_in = load(transfer, t)

    pl.semaphore_wait(
        barrier, 4 + 3 * has_north.astype(jnp.int32) + 3 * has_south.astype(jnp.int32)
    )

    count = [0]

    def remote(src, dst, to_lon, to_lat):
        n = count[0]
        count[0] += 1
        return pltpu.make_async_remote_copy(
            src_ref=src,
            dst_ref=dst,
            send_sem=send_sem.at[n],
            recv_sem=recv_sem.at[n],
            device_id=(to_lon, to_lat),
            device_id_type=MESH,
        )

    def columns(spans, source, target, to_lon):
        return [
            remote(source(pl.ds(k0, k1 - k0)), target(pl.ds(k0, k1 - k0)), to_lon, lat)
            for k0, k1 in spans
        ]

    def first_columns(plus, minus):
        return columns(
            plus, lambda k: spectrum.at[k, width - 1, :], lambda k: x.at[1, k, :], east
        ) + columns(minus, lambda k: spectrum.at[k, 0, :], lambda k: x.at[width + 2, k, :], west)

    head, rest = zip(split(plus, HEAD), split(minus, HEAD))
    first_head, first_rest = first_columns(*head), first_columns(*rest)
    first = first_head + first_rest
    second = columns(
        plus, lambda k: a.at[width, k, :], lambda k: a.at[0, k, :], east
    ) + columns(minus, lambda k: a.at[1, k, :], lambda k: a.at[width + 1, k, :], west)
    side_masks = [
        remote(sea.at[pl.ds(width - 1, 1), :], far_masks.at[0], east, lat),
        remote(sea.at[pl.ds(0, 1), :], far_masks.at[1], west, lat),
    ]
    for copy in side_masks + first_head:
        copy.start()

    for c in range(width):
        masks[c + 2] = jnp.broadcast_to(
            sea[pl.ds(c, 1), :].astype(jnp.float32), (PAIR, LANES)
        )

    for copy in columns_in:
        copy.wait()

    half = lane // 2
    edge_lanes = jnp.where(half < 8, LANES - 2, 0) + lane % 2

    def pack(r, values):
        total = jnp.zeros((PAIR, LANES), jnp.float32)
        for c in range(width):
            total = jnp.where(half % 8 == c, lanes_of(values[c], edge_lanes), total)
        packed[pl.ds(r, PAIR), :] = total

    def pack_rows(p):
        r = pl.multiple_of(p * PAIR, PAIR)
        values = []
        for c in range(width):
            value = x[c + 2, pl.ds(r, PAIR), :] * masks[c + 2]
            x[c + 2, pl.ds(r, PAIR), :] = value
            values.append(value)
        pack(r, values)

    repeat(components // PAIR, pack_rows, 9)
    pack(components, [masks[c + 2] for c in range(width)])
    blocks = packed.shape[0] // LANES
    tail = components + PAIR
    packed[pl.ds(tail, blocks * LANES - tail), :] = jnp.zeros(
        (blocks * LANES - tail, LANES), jnp.float32
    )
    for b in range(blocks):
        turned[:, b * LANES : (b + 1) * LANES] = jnp.transpose(
            packed[b * LANES : (b + 1) * LANES, :]
        )[:32, :]

    to_north = [
        remote(turned.at[pl.ds(0, 16), :], gturned.at[pl.ds(0, 16), :], lon, lat + 1),
        remote(turned.at[pl.ds(15, 1), :], gturned.at[pl.ds(32, 1), :], east, lat + 1),
        remote(turned.at[pl.ds(1, 1), :], gturned.at[pl.ds(33, 1), :], west, lat + 1),
    ]
    to_south = [
        remote(turned.at[pl.ds(16, 16), :], gturned.at[pl.ds(16, 16), :], lon, lat - 1),
        remote(turned.at[pl.ds(30, 1), :], gturned.at[pl.ds(34, 1), :], east, lat - 1),
        remote(turned.at[pl.ds(16, 1), :], gturned.at[pl.ds(35, 1), :], west, lat - 1),
    ]

    @pl.when(has_north)
    def _():
        for copy in to_north:
            copy.start()

    @pl.when(has_south)
    def _():
        for copy in to_south:
            copy.start()

    for copy in first_rest:
        copy.start()

    coef_in.wait()
    bulk_turned[...] = jnp.zeros_like(bulk_turned)
    for b in range(blocks):
        low = b * LANES
        high = min(low + LANES, components)
        bulk_turned[pl.ds(0, quantities), : high - low] = bulk_weight[:, low:high]
        part = jnp.transpose(bulk_turned[...])
        rows = pl.ds(low, high - low)
        for q in range(quantities):
            bulk_wide[q, rows, :] = jnp.broadcast_to(
                part[: high - low, q : q + 1], (high - low, LANES)
            )

    def widen(p):
        rows = pl.ds(pl.multiple_of(p * PAIR, PAIR), PAIR)
        line = coef[rows, :]
        for n in range(3):
            wide[n, rows, :] = jnp.broadcast_to(line[:, n : n + 1], (PAIR, LANES))

    repeat(components // PAIR, widen, 9)

    for copy in (cell_in, weight_in, u_in, v_in):
        copy.wait()
    height, taps, length = cell.shape
    for i in range(height):
        for tap in range(taps):
            cells[tap, pl.ds(i, 1), :] = cell[i, pl.ds(tap, 1), :]
            weights[tap, pl.ds(i, 1), :] = weight[i, pl.ds(tap, 1), :]
    levels = u.shape[0]
    for side, row in ((0, height - 1), (1, 0)):
        for level in range(levels):
            rows_send[side, pl.ds(level, 1), :] = u[level, pl.ds(row, 1), :]
            rows_send[side, pl.ds(levels + level, 1), :] = v[level, pl.ds(row, 1), :]
        for tap in range(taps):
            rows_send[side, pl.ds(2 * levels + tap, 1), :] = weights[tap, pl.ds(row, 1), :]
            rows_send[side, pl.ds(2 * levels + taps + tap, 1), :] = cells[
                tap, pl.ds(row, 1), :
            ].astype(jnp.float32)
    lane_all = lax.broadcasted_iota(jnp.int32, (height, LANES), 1)
    for side, start, source in ((0, length - LANES, LANES - 1), (1, 0, 0)):
        total = jnp.zeros((height, LANES), jnp.float32)
        for n in range(2 * levels + 2 * taps):
            if n < levels:
                block = u[n, :, start : start + LANES]
            elif n < 2 * levels:
                block = v[n - levels, :, start : start + LANES]
            elif n < 2 * levels + taps:
                block = weights[n - 2 * levels, :, start : start + LANES]
            else:
                block = cells[n - 2 * levels - taps, :, start : start + LANES].astype(jnp.float32)
            total = jnp.where(lane_all == n, lane_shift(block, source, n), total)
        cols_send[side] = total

    stores = []

    def store(src, dst):
        copy = pltpu.make_async_copy(src, dst, out_sem.at[len(stores)])
        copy.start()
        stores.append(copy)

    store(cells, cells_out)
    store(weights, weights_out)

    @pl.when(has_south)
    def _():
        for copy in to_north:
            copy.wait_recv()

    @pl.when(has_north)
    def _():
        for copy in to_south:
            copy.wait_recv()

    for b in range(blocks):
        g[b * LANES : (b + 1) * LANES, :] = jnp.transpose(
            gturned[:, b * LANES : (b + 1) * LANES]
        )
    inner = list(range(1, width - 1))
    outer = [0, width - 1]
    ghost_at = len(inner) * LANES

    def first_inner(r, xs, ys):
        co = coefficients(coef, wide, r, xs, ys)
        rows = pl.ds(r, PAIR)
        state = {c: x[c + 2, rows, :] for c in needed(inner, xs)}
        ghost = g[rows, :]
        mine = packed[rows, :]
        for c, value in advect_columns(co, xs, ys, inner, state, ghost, lane).items():
            a[c + 1, rows, :] = value
            ab[rows, (c - 1) * LANES : c * LANES] = value.astype(jnp.bfloat16)

        def sideways(step, low, high):
            moved = pltpu.roll(ghost, step % LANES, 1)
            for target, source in (low, high):
                moved = jnp.where(lane == target, lane_shift(ghost, source, target), moved)
            return moved

        value = upwind(
            co,
            xs,
            ys,
            ghost,
            lambda: sideways(2, (1, 32), (16, 34)),
            lambda: sideways(-2, (15, 33), (30, 35)),
            lambda: jnp.where(lane < 16, pltpu.roll(ghost, 1, 1), pltpu.roll(mine, 15, 1)),
            lambda: jnp.where(
                lane < 16, pltpu.roll(mine, LANES - 15, 1), pltpu.roll(ghost, LANES - 1, 1)
            ),
        )
        ga[rows, :] = value
        ab[rows, ghost_at : ghost_at + LANES] = value.astype(jnp.bfloat16)

    over_rows(runs, first_inner)
    transfer_in.wait()
    block = 432
    ghost_mask = g[pl.ds(components, 1), :]

    def inner_product(state, shift, with_ghost):
        def product(m, carry):
            rows = pl.ds(pl.multiple_of(m * block, PAIR), block)
            for n in range(0, len(inner), 2):
                added = jnp.dot(
                    t[rows, :],
                    ab[:, n * LANES : (n + 2) * LANES],
                    preferred_element_type=jnp.float32,
                )
                for c in (n + 1, n + 2):
                    part = added[:, (c - n - 1) * LANES : (c - n) * LANES]
                    state[c + shift, rows, :] = masks[c + 2, pl.ds(0, 1), :] * (
                        state[c + shift, rows, :] + 0.5 * part
                    )
            if with_ghost:
                added = jnp.dot(
                    t[rows, :],
                    ab[:, ghost_at : ghost_at + LANES],
                    preferred_element_type=jnp.float32,
                )
                ga[rows, :] = ghost_mask * (ga[rows, :] + 0.5 * added)
            return carry

        lax.fori_loop(0, components // block, product, 0)

    def outer_product(state, shift):
        def product(m, carry):
            rows = pl.ds(pl.multiple_of(m * block, PAIR), block)
            added = jnp.dot(t[rows, :], abe[...], preferred_element_type=jnp.float32)
            for n, c in enumerate(outer):
                part = added[:, n * LANES : (n + 1) * LANES]
                state[c + shift, rows, :] = masks[c + 2, pl.ds(0, 1), :] * (
                    state[c + shift, rows, :] + 0.5 * part
                )
            return carry

        lax.fori_loop(0, components // block, product, 0)

    inner_product(a, 1, True)

    for copy in side_masks + first:
        copy.wait_recv()
    for slot, side in ((1, 0), (width + 2, 1)):
        masks[slot] = jnp.broadcast_to(far_masks[side].astype(jnp.float32), (PAIR, LANES))

    def first_outer(r, xs, ys):
        co = coefficients(coef, wide, r, xs, ys)
        rows = pl.ds(r, PAIR)
        state = {}
        for c in needed(outer, xs):
            value = x[c + 2, rows, :]
            state[c] = value * masks[c + 2] if c in (-1, width) else value
        for n, (c, value) in enumerate(
            advect_columns(co, xs, ys, outer, state, g[rows, :], lane).items()
        ):
            a[c + 1, rows, :] = value
            abe[rows, n * LANES : (n + 1) * LANES] = value.astype(jnp.bfloat16)

    over_rows(runs, first_outer)
    outer_product(a, 1)
    for copy in second:
        copy.start()
    rows_copy = [
        remote(rows_send.at[0], rows_in.at[0], east, lat),
        remote(rows_send.at[1], rows_in.at[1], west, lat),
    ]
    cols_north = remote(cols_send.at[0], cols_in.at[0], lon, lat + 1)
    cols_south = remote(cols_send.at[1], cols_in.at[1], lon, lat - 1)
    for copy in rows_copy:
        copy.start()

    @pl.when(has_north)
    def _():
        cols_north.start()

    @pl.when(has_south)
    def _():
        cols_south.start()

    def second_step(group, target):
        def step(r, xs, ys):
            co = coefficients(coef, wide, r, xs, ys)
            rows = pl.ds(r, PAIR)
            state = {c: a[c + 1, rows, :] for c in needed(group, xs)}
            for n, (c, value) in enumerate(
                advect_columns(co, xs, ys, group, state, ga[rows, :], lane).items()
            ):
                x[c + 2, rows, :] = value
                target[rows, n * LANES : (n + 1) * LANES] = value.astype(jnp.bfloat16)

        over_rows(runs, step)

    for copy in side_masks + first:
        copy.wait_send()
    second_step(inner, ab)
    inner_product(x, 2, False)
    for c in inner:
        store(x.at[c + 2], s2_out.at[c])
    bulk_of(bulk_wide, x, inner, quantities, components, bulk)

    for copy in second:
        copy.wait_recv()
    second_step(outer, abe)
    outer_product(x, 2)
    for c in outer:
        store(x.at[c + 2], s2_out.at[c])
    bulk_of(bulk_wide, x, outer, quantities, components, bulk)

    drift = bulk.at[pl.ds(1, 2)]
    stress = bulk.at[pl.ds(0, 2)]
    flat = [
        remote(bulk, near.at[2], west, lat),
        remote(bulk, near.at[0], east, lat),
        remote(stress, far.at[1], around[0], lat),
        remote(stress, far.at[0], around[4], lat),
    ]
    spread_north = [
        remote(drift, sides.at[0, 2], west, lat + 1),
        remote(drift, sides.at[0, 1], lon, lat + 1),
        remote(drift, sides.at[0, 0], east, lat + 1),
    ]
    spread_south = [
        remote(drift, sides.at[1, 2], west, lat - 1),
        remote(drift, sides.at[1, 1], lon, lat - 1),
        remote(drift, sides.at[1, 0], east, lat - 1),
    ]
    for copy in flat:
        copy.start()

    @pl.when(has_north)
    def _():
        for copy in spread_north:
            copy.start()

    @pl.when(has_south)
    def _():
        for copy in spread_south:
            copy.start()

    near[1] = bulk[...]

    for copy in rows_copy:
        copy.wait()
    for copy in second:
        copy.wait_send()

    @pl.when(has_north)
    def _():
        for copy in to_north + [cols_north]:
            copy.wait_send()
        cols_south.wait_recv()

    @pl.when(has_south)
    def _():
        for copy in to_south + [cols_south]:
            copy.wait_send()
        cols_north.wait_recv()

    store(rows_in, rows_out)
    store(cols_in, cols_out)

    for copy in flat:
        copy.wait()

    @pl.when(has_north)
    def _():
        for copy in spread_north:
            copy.wait_send()
        for copy in spread_south:
            copy.wait_recv()

    @pl.when(has_south)
    def _():
        for copy in spread_south:
            copy.wait_send()
        for copy in spread_north:
            copy.wait_recv()

    store(near, near_out)
    store(sides, sides_out)
    store(far, far_out)
    for copy in stores:
        copy.wait()


def taken_from(sources, codes, quantities):
    taken = []
    for code in codes:
        place, offset = code & (LANES - 1), code >> 9
        values = [jnp.zeros(code.shape, jnp.float32)] * len(quantities)
        for o in range(17):
            hit = offset == o
            for n, q in enumerate(quantities):
                values[n] = jnp.where(hit, lanes_of(sources(q, o), place), values[n])
        taken.append(values)
    return taken


def ocean_kernel(
    s2, u, v, sea, near, sides, far, cells, weights, rows_in, cols_in, coriolis,
    spectrum_out, u_out, v_out,
    near1, near3, sides3, forcing, edge_code, edge_weight, edge_rows, out_sem,
):
    quantities = near.shape[1]
    width = near.shape[2]
    taps, height, length = cells.shape
    levels = u.shape[0]
    writes = [
        pltpu.make_async_copy(s2.at[c], spectrum_out.at[:, c, :], out_sem.at[c])
        for c in range(width)
    ]
    for copy in writes:
        copy.start()
    for part in range(3):
        near1[:, pl.ds(8 + part * width, width), :] = near[part]
    near1[pl.ds(0, 2), pl.ds(7, 1), :] = far[0, :, pl.ds(width - 1, 1), :]
    near1[pl.ds(0, 2), pl.ds(8 + 3 * width, 1), :] = far[1, :, pl.ds(0, 1), :]
    for i in range(3 * width):
        for q in range(quantities):
            near3[q, pl.ds(3 * i, 3), :] = jnp.broadcast_to(
                near1[q, pl.ds(8 + i, 1), :], (3, LANES)
            )
        for side in range(2):
            for q in range(2):
                sides3[side, q, pl.ds(3 * i, 3), :] = jnp.broadcast_to(
                    sides[side, i // width, q, pl.ds(i % width, 1), :], (3, LANES)
                )

    def block(jb):
        lanes = pl.ds(jb * LANES, LANES)
        for i0 in range(0, height, 8):
            rows = pl.ds(i0, 8)
            taken = taken_from(
                lambda q, o: near3[q, pl.ds(i0 + 3 * o, 8), :],
                [cells[tap, rows, lanes] for tap in range(taps)],
                range(quantities),
            )
            for q in range(quantities):
                total = 0.0
                for tap in range(taps):
                    total = total + taken[tap][q] * weights[tap, rows, lanes]
                forcing[q, rows, lanes] = total
        low = lax.broadcasted_iota(jnp.int32, (8, LANES), 0) < 4
        taken = taken_from(
            lambda q, o: jnp.where(
                low,
                jnp.broadcast_to(near1[q, pl.ds(7 + o, 1), :], (8, LANES)),
                jnp.broadcast_to(near1[q, pl.ds(16 + o, 1), :], (8, LANES)),
            ),
            [edge_code[:, lanes].astype(jnp.int32)],
            range(2),
        )
        for q in range(2):
            product = taken[0][q] * edge_weight[:, lanes]
            zero = jnp.zeros_like(product)
            edge_rows[q, pl.ds(0, 1), lanes] = jnp.sum(
                jnp.where(low, product, zero), axis=0, keepdims=True
            )
            edge_rows[q, pl.ds(1, 1), lanes] = jnp.sum(
                jnp.where(low, zero, product), axis=0, keepdims=True
            )

    for side in range(2):
        edge_code[pl.ds(4 * side, 4), :] = rows_in[side, pl.ds(2 * levels + taps, taps), :]
        edge_weight[pl.ds(4 * side, 4), :] = rows_in[side, pl.ds(2 * levels, taps), :]
    blocks = length // LANES
    for jb in range(blocks):
        block(jb)

    lane = lax.broadcasted_iota(jnp.int32, (8, LANES), 1)
    here = jnp.logical_and(lane >= 2 * levels + taps, lane < 2 * levels + 2 * taps)
    edge_cols = [[], []]
    for side in range(2):
        parts = [[], []]
        for i0 in range(0, height, 8):
            line = cols_in[side, pl.ds(i0, 8), :]
            code = jnp.where(here, line, 0.0).astype(jnp.int32)
            taken = taken_from(
                lambda q, o: sides3[side, q, pl.ds(i0 + 3 * o, 8), :], [code], range(2)
            )
            weight = jnp.where(here, pltpu.roll(line, taps, 1), 0.0)
            for q in range(2):
                parts[q].append(jnp.sum(taken[0][q] * weight, axis=1, keepdims=True))
        for q in range(2):
            edge_cols[side].append(jnp.concatenate(parts[q], axis=0))

    row = lax.broadcasted_iota(jnp.int32, (height, length), 0)
    col = lax.broadcasted_iota(jnp.int32, (height, length), 1)

    def shifted(q, west, east, south, north):
        return (
            jnp.where(row == 0, west, pltpu.roll(q, 1, 0)),
            jnp.where(row == height - 1, east, pltpu.roll(q, height - 1, 0)),
            jnp.where(col == 0, south, pltpu.roll(q, 1, 1)),
            jnp.where(col == length - 1, north, pltpu.roll(q, length - 1, 1)),
        )

    def dx(q, index):
        low = jnp.where(row == 0, edge_rows[index, pl.ds(0, 1), :], pltpu.roll(q, 1, 0))
        high = jnp.where(
            row == height - 1, edge_rows[index, pl.ds(1, 1), :], pltpu.roll(q, height - 1, 0)
        )
        return 0.5 * (high - low)

    def dy(q, index):
        low = jnp.where(col == 0, edge_cols[0][index], pltpu.roll(q, 1, 1))
        high = jnp.where(col == length - 1, edge_cols[1][index], pltpu.roll(q, length - 1, 1))
        return 0.5 * (high - low)

    sxx, sxy, syy = forcing[0], forcing[1], forcing[2]
    force_x = -(dx(sxx, 0) + dy(sxy, 0))
    force_y = -(dx(sxy, 1) + dy(syy, 1))
    wet = sea[...].astype(jnp.float32)
    turn = jnp.broadcast_to(0.5 * coriolis[...][None], (height, length))
    for level in range(levels):
        decay = math.exp(-level / 3.0)
        here_u, here_v = u[level], v[level]

        def laplace(q, n):
            west, east, south, north = shifted(
                q,
                rows_in[0, pl.ds(n, 1), :],
                rows_in[1, pl.ds(n, 1), :],
                cols_in[0, :, n : n + 1],
                cols_in[1, :, n : n + 1],
            )
            return east + west + north + south - 4.0 * q

        u_out[level] = wet * (
            here_u
            + turn * (here_v + decay * forcing[4])
            + (0.5 * decay) * force_x
            + 0.1 * laplace(here_u, level)
        )
        v_out[level] = wet * (
            here_v
            - turn * (here_u + decay * forcing[3])
            + (0.5 * decay) * force_y
            + 0.1 * laplace(here_v, levels + level)
        )
    for copy in writes:
        copy.wait()


def local(
    spectrum,
    sea_mask,
    transfer,
    bulk_weight,
    remap_cell,
    remap_weight,
    ocean_u,
    ocean_v,
    ocean_mask,
    coriolis,
):
    f32, i32 = jnp.float32, jnp.int32
    components, width, _ = spectrum.shape
    levels, height, length = ocean_u.shape
    taps = remap_cell.shape[2]
    quantities = bulk_weight.shape[0]
    padded = -(-(components + PAIR) // LANES) * LANES
    coef = courant(components, NFREQ)
    cell = jnp.transpose(remap_cell, (0, 2, 1))
    weight = jnp.transpose(remap_weight, (0, 2, 1))
    messages = 2 * levels + 2 * taps
    S = jax.ShapeDtypeStruct
    dma = pltpu.SemaphoreType.DMA
    near_shape = (3, quantities, width, LANES)
    sides_shape = (2, 3, 2, width, LANES)
    far_shape = (2, 2, width, LANES)
    s2, near, sides, far, cells, weights, rows_in, cols_in = pl.pallas_call(
        wave_kernel,
        name="wave",
        out_shape=(
            S((width, components, LANES), f32),
            S(near_shape, f32),
            S(sides_shape, f32),
            S(far_shape, f32),
            S((taps, height, length), i32),
            S((taps, height, length), f32),
            S((2, messages, length), f32),
            S((2, height, LANES), f32),
        ),
        in_specs=[HBM, VMEM, HBM, HBM, VMEM, HBM, HBM, HBM, HBM],
        out_specs=(ANY,) * 8,
        scratch_shapes=[
            pltpu.VMEM((width + 4, components, LANES), f32),
            pltpu.VMEM((width + 2, components, LANES), f32),
            pltpu.VMEM((components, (width - 1) * LANES), jnp.bfloat16),
            pltpu.VMEM((components, 2 * LANES), jnp.bfloat16),
            pltpu.VMEM((components, components), jnp.bfloat16),
            pltpu.VMEM((components, 8), f32),
            pltpu.VMEM((3, components, LANES), f32),
            pltpu.VMEM((LANES, LANES), f32),
            pltpu.VMEM((quantities, components, LANES), f32),
            pltpu.VMEM((width + 4, PAIR, LANES), f32),
            pltpu.VMEM((padded, LANES), f32),
            pltpu.VMEM((32, padded), f32),
            pltpu.VMEM((LANES, padded), f32),
            pltpu.VMEM((padded, LANES), f32),
            pltpu.VMEM((components, LANES), f32),
            pltpu.VMEM((height, taps, length), i32),
            pltpu.VMEM((height, taps, length), f32),
            pltpu.VMEM((levels, height, length), f32),
            pltpu.VMEM((levels, height, length), f32),
            pltpu.VMEM((taps, height, length), i32),
            pltpu.VMEM((taps, height, length), f32),
            pltpu.VMEM((2, messages, length), f32),
            pltpu.VMEM((2, height, LANES), f32),
            pltpu.VMEM((2, messages, length), f32),
            pltpu.VMEM((2, height, LANES), f32),
            pltpu.VMEM((quantities, width, LANES), f32),
            pltpu.VMEM(near_shape, f32),
            pltpu.VMEM(sides_shape, f32),
            pltpu.VMEM(far_shape, f32),
            pltpu.VMEM((2, 1, LANES), i32),
            dma((16,)),
            dma((32,)),
            dma((32,)),
            dma((16,)),
        ],
        compiler_params=pltpu.CompilerParams(
            collective_id=0, has_side_effects=True, vmem_limit_bytes=WAVE_GRANT
        ),
    )(
        *map(
            in_hbm,
            (
                spectrum, sea_mask, transfer, jnp.asarray(coef), bulk_weight, cell, weight,
                ocean_u, ocean_v,
            ),
        )
    )

    return pl.pallas_call(
        ocean_kernel,
        name="ocean",
        out_shape=(S(spectrum.shape, f32), S(ocean_u.shape, f32), S(ocean_v.shape, f32)),
        in_specs=[ANY] + [VMEM] * 11,
        out_specs=(HBM, VMEM, VMEM),
        scratch_shapes=[
            pltpu.VMEM((quantities, 8 + 3 * width + 8, LANES), f32),
            pltpu.VMEM((quantities, 9 * width, LANES), f32),
            pltpu.VMEM((2, 2, 9 * width, LANES), f32),
            pltpu.VMEM((quantities, height, length), f32),
            pltpu.VMEM((8, length), f32),
            pltpu.VMEM((8, length), f32),
            pltpu.VMEM((2, 8, length), f32),
            dma((width,)),
        ],
        compiler_params=pltpu.CompilerParams(vmem_limit_bytes=OCEAN_GRANT),
    )(
        s2, ocean_u, ocean_v, ocean_mask, near, sides, far, cells, weights, rows_in, cols_in,
        coriolis,
    )


def solution(mesh):
    placed = (
        P(None, "lon", "lat"),
        P("lon", "lat"),
        P(),
        P(),
        P("lon", "lat", None),
        P("lon", "lat", None),
        P(None, "lon", "lat"),
        P(None, "lon", "lat"),
        P("lon", "lat"),
        P("lat"),
    )
    return jax.shard_map(
        local,
        mesh=mesh,
        in_specs=placed,
        out_specs=(P(None, "lon", "lat"), P(None, "lon", "lat"), P(None, "lon", "lat")),
        check_vma=False,
    )
```

```python
import math

import jax
import jax.numpy as jnp
import numpy as np
from jax import lax
from jax.experimental import pallas as pl
from jax.experimental.pallas import tpu as pltpu
from jax.sharding import PartitionSpec as P

NFREQ = 36
MESH = pl.DeviceIdType.MESH
VMEM = pl.BlockSpec(memory_space=pltpu.VMEM)
ANY = pl.BlockSpec(memory_space=pl.ANY)
HBM = pl.BlockSpec(memory_space=pltpu.HBM)
LANES = 128
PAIR = 16
OCEAN_GRANT = 12000 * 1024
WAVE_GRANT = 40000 * 1024
PARTS = (((0, 256), (384, 640)), ((640, 896), (1024, 1296)), ((256, 384), (896, 1024)))


def courant(components, freqs):
    index = np.arange(components)
    theta = 2.0 * np.pi * (index // freqs + 0.5) / (components // freqs)
    speed = 1.1 ** -(index % freqs).astype(np.float64)
    east, north = 0.45 * speed * np.cos(theta), 0.45 * speed * np.sin(theta)
    parts = [1.0 - abs(east) - abs(north), abs(east), abs(north)]
    parts += [np.maximum(p, 0.0) for p in (east, -east, north, -north)] + [0.0 * east]
    return np.stack(parts, axis=1).astype(np.float32)


def sign_of(function, first, last, freqs, directions):
    signs = set()
    for d in range(first // freqs, (last - 1) // freqs + 1):
        signs.add(1 if function(2 * math.pi * (d + 0.5) / directions) > 0 else -1)
    return signs.pop() if len(signs) == 1 else 0


def in_hbm(value):
    return pltpu.with_memory_space_constraint(value, pltpu.HBM)


def segments(components, freqs):
    directions = components // freqs
    runs = []
    for pair in range(components // PAIR):
        first, last = pair * PAIR, (pair + 1) * PAIR
        key = (
            sign_of(math.cos, first, last, freqs, directions),
            sign_of(math.sin, first, last, freqs, directions),
        )
        if runs and runs[-1][2] == key:
            runs[-1][1] = pair + 1
        else:
            runs.append([pair, pair + 1, key])
    return [(a, b, xs, ys) for a, b, (xs, ys) in runs]


def row_spans(components, freqs, sign):
    spans = []
    for a, b, xs, _ in segments(components, freqs):
        if xs == -sign:
            continue
        if spans and spans[-1][1] == a * PAIR:
            spans[-1][1] = b * PAIR
        else:
            spans.append([a * PAIR, b * PAIR])
    return [tuple(s) for s in spans]


def overlap(spans, low, high):
    cut = [(max(a, low), min(b, high)) for a, b in spans]
    return [(a, b) for a, b in cut if a < b]


def clipped(runs, low, high):
    cut = [(max(a, low // PAIR), min(b, high // PAIR), xs, ys) for a, b, xs, ys in runs]
    return [run for run in cut if run[0] < run[1]]


def south_lane(c):
    return 2 * c + 1 if 0 <= c < 8 else (32 if c < 0 else 33)


def north_lane(c):
    return 16 + 2 * c if 0 <= c < 8 else (34 if c < 0 else 35)


def lane_shift(x, source, target):
    return pltpu.roll(x, (target - source) % LANES, 1)


def lanes_of(x, index):
    return jnp.take_along_axis(x, index, axis=1, mode="promise_in_bounds")


def coefficients(coef, wide, r, xs, ys):
    rows = pl.ds(r, PAIR)

    def spread(n):
        return jnp.broadcast_to(coef[rows, n : n + 1], (PAIR, LANES))

    return dict(
        c=wide[0, rows, :],
        x=wide[1, rows, :] if xs else (spread(3), spread(4)),
        y=wide[2, rows, :] if ys else (spread(5), spread(6)),
    )


def upwind(co, xs, ys, centre, west, east, south, north):
    result = co["c"] * centre
    if xs:
        result = result + co["x"] * (west() if xs > 0 else east())
    else:
        result = result + co["x"][0] * west() + co["x"][1] * east()
    if ys:
        result = result + co["y"] * (south() if ys > 0 else north())
    else:
        result = result + co["y"][0] * south() + co["y"][1] * north()
    return result


def advect_columns(co, xs, ys, columns, state, ghost, lane):
    out = {}
    for c in columns:
        out[c] = upwind(
            co,
            xs,
            ys,
            state[c],
            lambda: state[c - 1],
            lambda: state[c + 1],
            lambda: jnp.where(
                lane == 0, lane_shift(ghost, south_lane(c), 0), pltpu.roll(state[c], 1, 1)
            ),
            lambda: jnp.where(
                lane == LANES - 1,
                lane_shift(ghost, north_lane(c), LANES - 1),
                pltpu.roll(state[c], LANES - 1, 1),
            ),
        )
    return out


def needed(columns, xs):
    want = set(columns)
    if xs >= 0:
        want |= {c - 1 for c in columns}
    if xs <= 0:
        want |= {c + 1 for c in columns}
    return sorted(want)


def over_rows(runs, body, unroll=10):
    for a, b, xs, ys in runs:
        steps = (b - a) // unroll
        if steps > 1:

            def step(p, carry, a=a, xs=xs, ys=ys):
                for j in range(unroll):
                    body(pl.multiple_of((a + p * unroll + j) * PAIR, PAIR), xs, ys)
                return carry

            lax.fori_loop(0, steps, step, 0)
            a += steps * unroll
        for p in range(a, b):
            body(p * PAIR, xs, ys)


def repeat(count, body, unroll):
    def step(p, carry):
        for j in range(unroll):
            body(p * unroll + j)
        return carry

    lax.fori_loop(0, count // unroll, step, 0)
    for p in range(count // unroll * unroll, count):
        body(p)


def bulk_of(bulk_wide, state, columns, quantities, components, bulk):
    unroll = 9

    def gather(p, totals):
        totals = list(totals)
        for j in range(unroll):
            rows = pl.ds(pl.multiple_of((p * unroll + j) * 8, 8), 8)
            wide = [bulk_wide[q, rows, :] for q in range(quantities)]
            for n, c in enumerate(columns):
                value = state[c + 2, rows, :]
                for q in range(quantities):
                    at = n * quantities + q
                    totals[at] = totals[at] + wide[q] * value
        return tuple(totals)

    zero = jnp.zeros((8, LANES), jnp.float32)
    totals = lax.fori_loop(
        0, components // 8 // unroll, gather, (zero,) * (len(columns) * quantities)
    )
    for n, c in enumerate(columns):
        for q in range(quantities):
            bulk[q, pl.ds(c, 1), :] = jnp.sum(
                totals[n * quantities + q], axis=0, keepdims=True
            )


def wave_kernel(
    spectrum, sea, transfer, coef_hbm, bulk_weight, cell_hbm, weight_hbm, u_hbm, v_hbm,
    s2_out, near_out, sides_out, far_out, cells_out, weights_out, rows_out, cols_out,
    x, a, ab, abe, t, coef, wide, bulk_turned, bulk_wide, masks, packed, turned, gturned, g, ga,
    cell, weight, u, v, cells, weights, rows_send, cols_send, cols_in,
    bulk, far_masks, acc, local_sem, send_sem, recv_sem, out_sem,
):
    lon, lat = lax.axis_index("lon"), lax.axis_index("lat")
    nlon, nlat = lax.axis_size("lon"), lax.axis_size("lat")
    components, width, _ = spectrum.shape
    quantities = bulk_weight.shape[0]
    runs = segments(components, NFREQ)
    plus = row_spans(components, NFREQ, 1)
    minus = row_spans(components, NFREQ, -1)
    around = [lax.rem(lon + d + nlon, nlon) for d in (-2, -1, 0, 1, 2)]
    east, west = around[3], around[1]
    has_south, has_north = lat > 0, lat < nlat - 1
    lane = lax.broadcasted_iota(jnp.int32, (PAIR, LANES), 1)

    gturned[...] = jnp.zeros_like(gturned)
    cols_in[...] = jnp.zeros_like(cols_in)

    local = []

    def load(src, dst):
        copy = pltpu.make_async_copy(src, dst, local_sem.at[len(local)])
        copy.start()
        local.append(copy)
        return copy

    barrier = pltpu.get_barrier_semaphore()

    def greet(to_lon, to_lat):
        pl.semaphore_signal(barrier, inc=1, device_id=(to_lon, to_lat), device_id_type=MESH)

    for d in (0, 1, 3, 4):
        greet(around[d], lat)

    @pl.when(has_north)
    def _():
        for d in (1, 2, 3):
            greet(around[d], lat + 1)

    @pl.when(has_south)
    def _():
        for d in (1, 2, 3):
            greet(around[d], lat - 1)

    columns_in = [load(spectrum.at[:, c, :], x.at[c + 2]) for c in range(width)]
    coef_in = load(coef_hbm, coef)
    cell_in = load(cell_hbm, cell)
    weight_in = load(weight_hbm, weight)
    u_in = load(u_hbm, u)
    v_in = load(v_hbm, v)
    transfer_in = load(transfer, t)

    pl.semaphore_wait(
        barrier, 4 + 3 * has_north.astype(jnp.int32) + 3 * has_south.astype(jnp.int32)
    )

    count = [0]

    def remote(src, dst, to_lon, to_lat):
        n = count[0]
        count[0] += 1
        return pltpu.make_async_remote_copy(
            src_ref=src,
            dst_ref=dst,
            send_sem=send_sem.at[n],
            recv_sem=recv_sem.at[n],
            device_id=(to_lon, to_lat),
            device_id_type=MESH,
        )

    def columns(spans, source, target, to_lon):
        return [
            remote(source(pl.ds(k0, k1 - k0)), target(pl.ds(k0, k1 - k0)), to_lon, lat)
            for k0, k1 in spans
        ]

    def both_ways(part, east_source, east_target, west_source, west_target):
        copies = []
        for low, high in part:
            copies += columns(overlap(plus, low, high), east_source, east_target, east)
            copies += columns(overlap(minus, low, high), west_source, west_target, west)
        return copies

    first = [
        both_ways(
            part,
            lambda k: spectrum.at[k, width - 1, :],
            lambda k: x.at[1, k, :],
            lambda k: spectrum.at[k, 0, :],
            lambda k: x.at[width + 2, k, :],
        )
        for part in PARTS
    ]
    second = [
        both_ways(
            part,
            lambda k: a.at[width, k, :],
            lambda k: a.at[0, k, :],
            lambda k: a.at[1, k, :],
            lambda k: a.at[width + 1, k, :],
        )
        for part in PARTS
    ]
    side_masks = [
        remote(sea.at[pl.ds(width - 1, 1), :], far_masks.at[0], east, lat),
        remote(sea.at[pl.ds(0, 1), :], far_masks.at[1], west, lat),
    ]
    for copy in side_masks + first[0]:
        copy.start()

    for c in range(width):
        masks[c + 2] = jnp.broadcast_to(
            sea[pl.ds(c, 1), :].astype(jnp.float32), (PAIR, LANES)
        )

    for copy in columns_in:
        copy.wait()

    half = lane // 2
    edge_lanes = jnp.where(half < 8, LANES - 2, 0) + lane % 2

    def pack(r, values):
        total = jnp.zeros((PAIR, LANES), jnp.float32)
        for c in range(width):
            total = jnp.where(half % 8 == c, lanes_of(values[c], edge_lanes), total)
        packed[pl.ds(r, PAIR), :] = total

    def pack_rows(p):
        r = pl.multiple_of(p * PAIR, PAIR)
        values = []
        for c in range(width):
            value = x[c + 2, pl.ds(r, PAIR), :] * masks[c + 2]
            x[c + 2, pl.ds(r, PAIR), :] = value
            values.append(value)
        pack(r, values)

    repeat(components // PAIR, pack_rows, 9)
    pack(components, [masks[c + 2] for c in range(width)])
    blocks = packed.shape[0] // LANES
    tail = components + PAIR
    packed[pl.ds(tail, blocks * LANES - tail), :] = jnp.zeros(
        (blocks * LANES - tail, LANES), jnp.float32
    )
    for b in range(blocks):
        turned[:, b * LANES : (b + 1) * LANES] = jnp.transpose(
            packed[b * LANES : (b + 1) * LANES, :]
        )[:32, :]

    to_north = [
        remote(turned.at[pl.ds(0, 16), :], gturned.at[pl.ds(0, 16), :], lon, lat + 1),
        remote(turned.at[pl.ds(15, 1), :], gturned.at[pl.ds(32, 1), :], east, lat + 1),
        remote(turned.at[pl.ds(1, 1), :], gturned.at[pl.ds(33, 1), :], west, lat + 1),
    ]
    to_south = [
        remote(turned.at[pl.ds(16, 16), :], gturned.at[pl.ds(16, 16), :], lon, lat - 1),
        remote(turned.at[pl.ds(30, 1), :], gturned.at[pl.ds(34, 1), :], east, lat - 1),
        remote(turned.at[pl.ds(16, 1), :], gturned.at[pl.ds(35, 1), :], west, lat - 1),
    ]

    @pl.when(has_north)
    def _():
        for copy in to_north:
            copy.start()

    @pl.when(has_south)
    def _():
        for copy in to_south:
            copy.start()

    for copy in first[1] + first[2]:
        copy.start()

    coef_in.wait()
    bulk_turned[...] = jnp.zeros_like(bulk_turned)
    for b in range(blocks):
        low = b * LANES
        high = min(low + LANES, components)
        bulk_turned[pl.ds(0, quantities), : high - low] = bulk_weight[:, low:high]
        part = jnp.transpose(bulk_turned[...])
        rows = pl.ds(low, high - low)
        for q in range(quantities):
            bulk_wide[q, rows, :] = jnp.broadcast_to(
                part[: high - low, q : q + 1], (high - low, LANES)
            )

    def widen(p):
        rows = pl.ds(pl.multiple_of(p * PAIR, PAIR), PAIR)
        line = coef[rows, :]
        for n in range(3):
            wide[n, rows, :] = jnp.broadcast_to(line[:, n : n + 1], (PAIR, LANES))

    repeat(components // PAIR, widen, 9)

    for copy in (cell_in, weight_in, u_in, v_in):
        copy.wait()
    height, taps, length = cell.shape
    for i in range(height):
        for tap in range(taps):
            cells[tap, pl.ds(i, 1), :] = cell[i, pl.ds(tap, 1), :]
            weights[tap, pl.ds(i, 1), :] = weight[i, pl.ds(tap, 1), :]
    levels = u.shape[0]
    for side, row in ((0, height - 1), (1, 0)):
        for level in range(levels):
            rows_send[side, pl.ds(level, 1), :] = u[level, pl.ds(row, 1), :]
            rows_send[side, pl.ds(levels + level, 1), :] = v[level, pl.ds(row, 1), :]
        for tap in range(taps):
            rows_send[side, pl.ds(2 * levels + tap, 1), :] = weights[tap, pl.ds(row, 1), :]
            rows_send[side, pl.ds(2 * levels + taps + tap, 1), :] = cells[
                tap, pl.ds(row, 1), :
            ].astype(jnp.float32)
    lane_all = lax.broadcasted_iota(jnp.int32, (height, LANES), 1)
    for side, start, source in ((0, length - LANES, LANES - 1), (1, 0, 0)):
        total = jnp.zeros((height, LANES), jnp.float32)
        for n in range(2 * levels + 2 * taps):
            if n < levels:
                block = u[n, :, start : start + LANES]
            elif n < 2 * levels:
                block = v[n - levels, :, start : start + LANES]
            elif n < 2 * levels + taps:
                block = weights[n - 2 * levels, :, start : start + LANES]
            else:
                block = cells[n - 2 * levels - taps, :, start : start + LANES].astype(jnp.float32)
            total = jnp.where(lane_all == n, lane_shift(block, source, n), total)
        cols_send[side] = total

    stores = []

    def store(src, dst):
        copy = pltpu.make_async_copy(src, dst, out_sem.at[len(stores)])
        copy.start()
        stores.append(copy)

    store(cells, cells_out)
    store(weights, weights_out)

    @pl.when(has_south)
    def _():
        for copy in to_north:
            copy.wait_recv()

    @pl.when(has_north)
    def _():
        for copy in to_south:
            copy.wait_recv()

    for b in range(blocks):
        g[b * LANES : (b + 1) * LANES, :] = jnp.transpose(
            gturned[:, b * LANES : (b + 1) * LANES]
        )
    inner = list(range(1, width - 1))
    outer = [0, width - 1]
    ghost_at = len(inner) * LANES

    def first_inner(r, xs, ys):
        co = coefficients(coef, wide, r, xs, ys)
        rows = pl.ds(r, PAIR)
        state = {c: x[c + 2, rows, :] for c in needed(inner, xs)}
        ghost = g[rows, :]
        mine = packed[rows, :]
        for c, value in advect_columns(co, xs, ys, inner, state, ghost, lane).items():
            a[c + 1, rows, :] = value
            ab[rows, (c - 1) * LANES : c * LANES] = value.astype(jnp.bfloat16)

        def sideways(step, low, high):
            moved = pltpu.roll(ghost, step % LANES, 1)
            for target, source in (low, high):
                moved = jnp.where(lane == target, lane_shift(ghost, source, target), moved)
            return moved

        value = upwind(
            co,
            xs,
            ys,
            ghost,
            lambda: sideways(2, (1, 32), (16, 34)),
            lambda: sideways(-2, (15, 33), (30, 35)),
            lambda: jnp.where(lane < 16, pltpu.roll(ghost, 1, 1), pltpu.roll(mine, 15, 1)),
            lambda: jnp.where(
                lane < 16, pltpu.roll(mine, LANES - 15, 1), pltpu.roll(ghost, LANES - 1, 1)
            ),
        )
        ga[rows, :] = value
        ab[rows, ghost_at : ghost_at + LANES] = value.astype(jnp.bfloat16)

    over_rows(runs, first_inner)
    block = 432
    ghost_mask = g[pl.ds(components, 1), :]

    def inner_product(state, shift, with_ghost):
        def product(m, carry):
            rows = pl.ds(pl.multiple_of(m * block, PAIR), block)
            for n in range(0, len(inner), 2):
                added = jnp.dot(
                    t[rows, :],
                    ab[:, n * LANES : (n + 2) * LANES],
                    preferred_element_type=jnp.float32,
                )
                for c in (n + 1, n + 2):
                    part = added[:, (c - n - 1) * LANES : (c - n) * LANES]
                    state[c + shift, rows, :] = masks[c + 2, pl.ds(0, 1), :] * (
                        state[c + shift, rows, :] + 0.5 * part
                    )
            if with_ghost:
                added = jnp.dot(
                    t[rows, :],
                    ab[:, ghost_at : ghost_at + LANES],
                    preferred_element_type=jnp.float32,
                )
                ga[rows, :] = ghost_mask * (ga[rows, :] + 0.5 * added)
            return carry

        lax.fori_loop(0, components // block, product, 0)

    def outer_part(index, advect_rows, state, shift):
        part = PARTS[index]
        for low, high in part:
            over_rows(clipped(runs, low, high), advect_rows, 8)

        def product(m, carry):
            rows = pl.ds(pl.multiple_of(m * block, PAIR), block)
            added = sum(
                jnp.dot(
                    t[rows, low:high], abe[low:high, :], preferred_element_type=jnp.float32
                )
                for low, high in part
            )
            if index:
                added = added + acc[rows, :]
            if index < len(PARTS) - 1:
                acc[rows, :] = added
            else:
                for n, c in enumerate(outer):
                    wet = masks[c + 2, pl.ds(0, 1), :]
                    state[c + shift, rows, :] = wet * (
                        state[c + shift, rows, :] + 0.5 * added[:, n * LANES : (n + 1) * LANES]
                    )
            return carry

        lax.fori_loop(0, components // block, product, 0)


    for copy in side_masks:
        copy.wait_recv()
    for slot, side in ((1, 0), (width + 2, 1)):
        masks[slot] = jnp.broadcast_to(far_masks[side].astype(jnp.float32), (PAIR, LANES))

    def first_outer(r, xs, ys):
        co = coefficients(coef, wide, r, xs, ys)
        rows = pl.ds(r, PAIR)
        state = {}
        for c in needed(outer, xs):
            value = x[c + 2, rows, :]
            state[c] = value * masks[c + 2] if c in (-1, width) else value
        for n, (c, value) in enumerate(
            advect_columns(co, xs, ys, outer, state, g[rows, :], lane).items()
        ):
            a[c + 1, rows, :] = value
            abe[rows, n * LANES : (n + 1) * LANES] = value.astype(jnp.bfloat16)

    transfer_in.wait()
    for index, copies in enumerate(first):
        for copy in copies:
            copy.wait_recv()
        outer_part(index, first_outer, a, 1)
    for copies in second:
        for copy in copies:
            copy.start()
    rows_copy = [
        remote(rows_send.at[0], rows_out.at[0], east, lat),
        remote(rows_send.at[1], rows_out.at[1], west, lat),
    ]
    cols_north = remote(cols_send.at[0], cols_in.at[0], lon, lat + 1)
    cols_south = remote(cols_send.at[1], cols_in.at[1], lon, lat - 1)
    for copy in rows_copy:
        copy.start()

    @pl.when(has_north)
    def _():
        cols_north.start()

    @pl.when(has_south)
    def _():
        cols_south.start()

    inner_product(a, 1, True)

    def second_step(group, target):
        def step(r, xs, ys):
            co = coefficients(coef, wide, r, xs, ys)
            rows = pl.ds(r, PAIR)
            state = {c: a[c + 1, rows, :] for c in needed(group, xs)}
            for n, (c, value) in enumerate(
                advect_columns(co, xs, ys, group, state, ga[rows, :], lane).items()
            ):
                x[c + 2, rows, :] = value
                target[rows, n * LANES : (n + 1) * LANES] = value.astype(jnp.bfloat16)

        return step

    for copies in [side_masks] + first:
        for copy in copies:
            copy.wait_send()
    over_rows(runs, second_step(inner, ab))
    inner_product(x, 2, False)
    for c in inner:
        store(x.at[c + 2], s2_out.at[c])
    bulk_of(bulk_wide, x, inner, quantities, components, bulk)

    for index, copies in enumerate(second):
        for copy in copies:
            copy.wait_recv()
        outer_part(index, second_step(outer, abe), x, 2)
    for c in outer:
        store(x.at[c + 2], s2_out.at[c])
    bulk_of(bulk_wide, x, outer, quantities, components, bulk)

    drift = bulk.at[pl.ds(1, 2)]
    stress = bulk.at[pl.ds(0, 2)]
    flat = [
        remote(bulk, near_out.at[2], west, lat),
        remote(bulk, near_out.at[0], east, lat),
        remote(stress, far_out.at[1], around[0], lat),
        remote(stress, far_out.at[0], around[4], lat),
    ]
    spread_north = [
        remote(drift, sides_out.at[0, 2], west, lat + 1),
        remote(drift, sides_out.at[0, 1], lon, lat + 1),
        remote(drift, sides_out.at[0, 0], east, lat + 1),
    ]
    spread_south = [
        remote(drift, sides_out.at[1, 2], west, lat - 1),
        remote(drift, sides_out.at[1, 1], lon, lat - 1),
        remote(drift, sides_out.at[1, 0], east, lat - 1),
    ]
    for copy in flat:
        copy.start()

    @pl.when(has_north)
    def _():
        for copy in spread_north:
            copy.start()

    @pl.when(has_south)
    def _():
        for copy in spread_south:
            copy.start()

    store(bulk, near_out.at[1])

    for copy in rows_copy:
        copy.wait()
    for copies in second:
        for copy in copies:
            copy.wait_send()

    @pl.when(has_north)
    def _():
        for copy in to_north + [cols_north]:
            copy.wait_send()
        cols_south.wait_recv()

    @pl.when(has_south)
    def _():
        for copy in to_south + [cols_south]:
            copy.wait_send()
        cols_north.wait_recv()

    store(cols_in, cols_out)

    for copy in flat:
        copy.wait()

    @pl.when(has_north)
    def _():
        for copy in spread_north:
            copy.wait_send()
        for copy in spread_south:
            copy.wait_recv()

    @pl.when(has_south)
    def _():
        for copy in spread_south:
            copy.wait_send()
        for copy in spread_north:
            copy.wait_recv()

    for copy in stores:
        copy.wait()


def taken_from(sources, codes, quantities):
    taken = []
    for code in codes:
        place, offset = code & (LANES - 1), code >> 9
        values = [jnp.zeros(code.shape, jnp.float32)] * len(quantities)
        for o in range(17):
            hit = offset == o
            for n, q in enumerate(quantities):
                values[n] = jnp.where(hit, lanes_of(sources(q, o), place), values[n])
        taken.append(values)
    return taken


def ocean_kernel(
    s2, u, v, sea, near, sides, far, cells, weights, rows_in, cols_in, coriolis,
    spectrum_out, u_out, v_out,
    near1, near3, sides3, forcing, edge_code, edge_weight, edge_rows, new_u, new_v, out_sem,
):
    quantities = near.shape[1]
    width = near.shape[2]
    taps, height, length = cells.shape
    levels = u.shape[0]
    writes = [
        pltpu.make_async_copy(s2.at[c], spectrum_out.at[:, c, :], out_sem.at[c])
        for c in range(width)
    ]
    for copy in writes:
        copy.start()
    for part in range(3):
        near1[:, pl.ds(8 + part * width, width), :] = near[part]
    near1[pl.ds(0, 2), pl.ds(7, 1), :] = far[0, :, pl.ds(width - 1, 1), :]
    near1[pl.ds(0, 2), pl.ds(8 + 3 * width, 1), :] = far[1, :, pl.ds(0, 1), :]
    for i in range(3 * width):
        for q in range(quantities):
            near3[q, pl.ds(3 * i, 3), :] = jnp.broadcast_to(
                near1[q, pl.ds(8 + i, 1), :], (3, LANES)
            )
        for side in range(2):
            for q in range(2):
                sides3[side, q, pl.ds(3 * i, 3), :] = jnp.broadcast_to(
                    sides[side, i // width, q, pl.ds(i % width, 1), :], (3, LANES)
                )

    def block(jb):
        lanes = pl.ds(jb * LANES, LANES)
        for i0 in range(0, height, 8):
            rows = pl.ds(i0, 8)
            taken = taken_from(
                lambda q, o: near3[q, pl.ds(i0 + 3 * o, 8), :],
                [cells[tap, rows, lanes] for tap in range(taps)],
                range(quantities),
            )
            for q in range(quantities):
                total = 0.0
                for tap in range(taps):
                    total = total + taken[tap][q] * weights[tap, rows, lanes]
                forcing[q, rows, lanes] = total
        low = lax.broadcasted_iota(jnp.int32, (8, LANES), 0) < 4
        taken = taken_from(
            lambda q, o: jnp.where(
                low,
                jnp.broadcast_to(near1[q, pl.ds(7 + o, 1), :], (8, LANES)),
                jnp.broadcast_to(near1[q, pl.ds(16 + o, 1), :], (8, LANES)),
            ),
            [edge_code[:, lanes].astype(jnp.int32)],
            range(2),
        )
        for q in range(2):
            product = taken[0][q] * edge_weight[:, lanes]
            zero = jnp.zeros_like(product)
            edge_rows[q, pl.ds(0, 1), lanes] = jnp.sum(
                jnp.where(low, product, zero), axis=0, keepdims=True
            )
            edge_rows[q, pl.ds(1, 1), lanes] = jnp.sum(
                jnp.where(low, zero, product), axis=0, keepdims=True
            )

    for side in range(2):
        edge_code[pl.ds(4 * side, 4), :] = rows_in[side, pl.ds(2 * levels + taps, taps), :]
        edge_weight[pl.ds(4 * side, 4), :] = rows_in[side, pl.ds(2 * levels, taps), :]
    blocks = length // LANES
    for jb in range(blocks):
        block(jb)

    lane = lax.broadcasted_iota(jnp.int32, (8, LANES), 1)
    here = jnp.logical_and(lane >= 2 * levels + taps, lane < 2 * levels + 2 * taps)
    edge_cols = [[], []]
    lat = lax.axis_index("lat")
    present = (lat > 0, lat < lax.axis_size("lat") - 1)
    for side in range(2):
        parts = [[], []]
        for i0 in range(0, height, 8):
            line = cols_in[side, pl.ds(i0, 8), :]
            code = jnp.where(here, line, 0.0).astype(jnp.int32)
            taken = taken_from(
                lambda q, o: sides3[side, q, pl.ds(i0 + 3 * o, 8), :], [code], range(2)
            )
            weight = jnp.where(here, pltpu.roll(line, taps, 1), 0.0)
            for q in range(2):
                value = jnp.sum(taken[0][q] * weight, axis=1, keepdims=True)
                parts[q].append(jnp.where(present[side], value, 0.0))
        for q in range(2):
            edge_cols[side].append(jnp.concatenate(parts[q], axis=0))

    row = lax.broadcasted_iota(jnp.int32, (height, length), 0)
    col = lax.broadcasted_iota(jnp.int32, (height, length), 1)

    def shifted(q, west, east, south, north):
        return (
            jnp.where(row == 0, west, pltpu.roll(q, 1, 0)),
            jnp.where(row == height - 1, east, pltpu.roll(q, height - 1, 0)),
            jnp.where(col == 0, south, pltpu.roll(q, 1, 1)),
            jnp.where(col == length - 1, north, pltpu.roll(q, length - 1, 1)),
        )

    def dx(q, index):
        low = jnp.where(row == 0, edge_rows[index, pl.ds(0, 1), :], pltpu.roll(q, 1, 0))
        high = jnp.where(
            row == height - 1, edge_rows[index, pl.ds(1, 1), :], pltpu.roll(q, height - 1, 0)
        )
        return 0.5 * (high - low)

    def dy(q, index):
        low = jnp.where(col == 0, edge_cols[0][index], pltpu.roll(q, 1, 1))
        high = jnp.where(col == length - 1, edge_cols[1][index], pltpu.roll(q, length - 1, 1))
        return 0.5 * (high - low)

    sxx, sxy, syy = forcing[0], forcing[1], forcing[2]
    force_x = -(dx(sxx, 0) + dy(sxy, 0))
    force_y = -(dx(sxy, 1) + dy(syy, 1))
    wet = sea[...].astype(jnp.float32)
    turn = jnp.broadcast_to(0.5 * coriolis[...][None], (height, length))
    for level in range(levels):
        decay = math.exp(-level / 3.0)
        here_u, here_v = u[level], v[level]

        def laplace(q, n):
            west, east, south, north = shifted(
                q,
                rows_in[0, pl.ds(n, 1), :],
                rows_in[1, pl.ds(n, 1), :],
                cols_in[0, :, n : n + 1],
                cols_in[1, :, n : n + 1],
            )
            return east + west + north + south - 4.0 * q

        new_u[level] = wet * (
            here_u
            + turn * (here_v + decay * forcing[4])
            + (0.5 * decay) * force_x
            + 0.1 * laplace(here_u, level)
        )
        new_v[level] = wet * (
            here_v
            - turn * (here_u + decay * forcing[3])
            + (0.5 * decay) * force_y
            + 0.1 * laplace(here_v, levels + level)
        )
        for n, (src, dst) in enumerate(((new_u, u_out), (new_v, v_out))):
            copy = pltpu.make_async_copy(
                src.at[level], dst.at[level], out_sem.at[width + n * levels + level]
            )
            copy.start()
            writes.append(copy)
    for copy in writes:
        copy.wait()


def local(
    spectrum,
    sea_mask,
    transfer,
    bulk_weight,
    remap_cell,
    remap_weight,
    ocean_u,
    ocean_v,
    ocean_mask,
    coriolis,
):
    f32, i32 = jnp.float32, jnp.int32
    components, width, _ = spectrum.shape
    levels, height, length = ocean_u.shape
    taps = remap_cell.shape[2]
    quantities = bulk_weight.shape[0]
    padded = -(-(components + PAIR) // LANES) * LANES
    coef = courant(components, NFREQ)
    cell = jnp.transpose(remap_cell, (0, 2, 1))
    weight = jnp.transpose(remap_weight, (0, 2, 1))
    messages = 2 * levels + 2 * taps
    S = jax.ShapeDtypeStruct
    dma = pltpu.SemaphoreType.DMA
    near_shape = (3, quantities, width, LANES)
    sides_shape = (2, 3, 2, width, LANES)
    far_shape = (2, 2, width, LANES)
    s2, near, sides, far, cells, weights, rows_in, cols_in = pl.pallas_call(
        wave_kernel,
        name="wave",
        out_shape=(
            S((width, components, LANES), f32),
            S(near_shape, f32),
            S(sides_shape, f32),
            S(far_shape, f32),
            S((taps, height, length), i32),
            S((taps, height, length), f32),
            S((2, messages, length), f32),
            S((2, height, LANES), f32),
        ),
        in_specs=[HBM, VMEM, HBM, HBM, VMEM, HBM, HBM, HBM, HBM],
        out_specs=(ANY,) * 8,
        scratch_shapes=[
            pltpu.VMEM((width + 4, components, LANES), f32),
            pltpu.VMEM((width + 2, components, LANES), f32),
            pltpu.VMEM((components, (width - 1) * LANES), jnp.bfloat16),
            pltpu.VMEM((components, 2 * LANES), jnp.bfloat16),
            pltpu.VMEM((components, components), jnp.bfloat16),
            pltpu.VMEM((components, 8), f32),
            pltpu.VMEM((3, components, LANES), f32),
            pltpu.VMEM((LANES, LANES), f32),
            pltpu.VMEM((quantities, components, LANES), f32),
            pltpu.VMEM((width + 4, PAIR, LANES), f32),
            pltpu.VMEM((padded, LANES), f32),
            pltpu.VMEM((32, padded), f32),
            pltpu.VMEM((LANES, padded), f32),
            pltpu.VMEM((padded, LANES), f32),
            pltpu.VMEM((components, LANES), f32),
            pltpu.VMEM((height, taps, length), i32),
            pltpu.VMEM((height, taps, length), f32),
            pltpu.VMEM((levels, height, length), f32),
            pltpu.VMEM((levels, height, length), f32),
            pltpu.VMEM((taps, height, length), i32),
            pltpu.VMEM((taps, height, length), f32),
            pltpu.VMEM((2, messages, length), f32),
            pltpu.VMEM((2, height, LANES), f32),
            pltpu.VMEM((2, height, LANES), f32),
            pltpu.VMEM((quantities, width, LANES), f32),
            pltpu.VMEM((2, 1, LANES), i32),
            pltpu.VMEM((components, 2 * LANES), f32),
            dma((16,)),
            dma((40,)),
            dma((40,)),
            dma((16,)),
        ],
        compiler_params=pltpu.CompilerParams(
            collective_id=0, has_side_effects=True, vmem_limit_bytes=WAVE_GRANT
        ),
    )(
        *map(
            in_hbm,
            (
                spectrum, sea_mask, transfer, jnp.asarray(coef), bulk_weight, cell, weight,
                ocean_u, ocean_v,
            ),
        )
    )

    return pl.pallas_call(
        ocean_kernel,
        name="ocean",
        out_shape=(S(spectrum.shape, f32), S(ocean_u.shape, f32), S(ocean_v.shape, f32)),
        in_specs=[ANY] + [VMEM] * 11,
        out_specs=(HBM, HBM, HBM),
        scratch_shapes=[
            pltpu.VMEM((quantities, 8 + 3 * width + 8, LANES), f32),
            pltpu.VMEM((quantities, 9 * width, LANES), f32),
            pltpu.VMEM((2, 2, 9 * width, LANES), f32),
            pltpu.VMEM((quantities, height, length), f32),
            pltpu.VMEM((8, length), f32),
            pltpu.VMEM((8, length), f32),
            pltpu.VMEM((2, 8, length), f32),
            pltpu.VMEM(ocean_u.shape, f32),
            pltpu.VMEM(ocean_v.shape, f32),
            dma((width + 2 * levels,)),
        ],
        compiler_params=pltpu.CompilerParams(vmem_limit_bytes=OCEAN_GRANT),
    )(
        s2, ocean_u, ocean_v, ocean_mask, near, sides, far, cells, weights, rows_in, cols_in,
        coriolis,
    )


def solution(mesh):
    placed = (
        P(None, "lon", "lat"),
        P("lon", "lat"),
        P(),
        P(),
        P("lon", "lat", None),
        P("lon", "lat", None),
        P(None, "lon", "lat"),
        P(None, "lon", "lat"),
        P("lon", "lat"),
        P("lat"),
    )
    return jax.shard_map(
        local,
        mesh=mesh,
        in_specs=placed,
        out_specs=(P(None, "lon", "lat"), P(None, "lon", "lat"), P(None, "lon", "lat")),
        check_vma=False,
    )
```

```python
import functools
import math

import jax
import jax.numpy as jnp
import numpy as np
from jax import lax
from jax.experimental import pallas as pl
from jax.experimental.pallas import tpu as pltpu
from jax.sharding import PartitionSpec as P

NFREQ = 36
MESH = pl.DeviceIdType.MESH
VMEM = pl.BlockSpec(memory_space=pltpu.VMEM)
ANY = pl.BlockSpec(memory_space=pl.ANY)
HBM = pl.BlockSpec(memory_space=pltpu.HBM)
LANES = 128
PAIR = 16
OCEAN_GRANT = 12000 * 1024
WAVE_GRANT = 40000 * 1024
PARTS = (((0, 256), (384, 640)), ((640, 896), (1024, 1296)), ((256, 384), (896, 1024)))
LAST = sum(high - low for low, high in PARTS[-1])
HEAD = ((0, 128), (384, 512))
BEHIND = ((128, 256), (512, 640))


def courant(components, freqs):
    index = np.arange(components)
    theta = 2.0 * np.pi * (index // freqs + 0.5) / (components // freqs)
    speed = 1.1 ** -(index % freqs).astype(np.float64)
    east, north = 0.45 * speed * np.cos(theta), 0.45 * speed * np.sin(theta)
    parts = [1.0 - abs(east) - abs(north), abs(east), abs(north)]
    parts += [np.maximum(p, 0.0) for p in (east, -east, north, -north)] + [0.0 * east]
    return np.stack(parts, axis=1).astype(np.float32)


def sign_of(function, first, last, freqs, directions):
    signs = set()
    for d in range(first // freqs, (last - 1) // freqs + 1):
        signs.add(1 if function(2 * math.pi * (d + 0.5) / directions) > 0 else -1)
    return signs.pop() if len(signs) == 1 else 0


def in_hbm(value):
    return pltpu.with_memory_space_constraint(value, pltpu.HBM)


def segments(components, freqs):
    directions = components // freqs
    runs = []
    for pair in range(components // PAIR):
        first, last = pair * PAIR, (pair + 1) * PAIR
        key = (
            sign_of(math.cos, first, last, freqs, directions),
            sign_of(math.sin, first, last, freqs, directions),
        )
        if runs and runs[-1][2] == key:
            runs[-1][1] = pair + 1
        else:
            runs.append([pair, pair + 1, key])
    return [(a, b, xs, ys) for a, b, (xs, ys) in runs]


def row_spans(components, freqs, sign):
    spans = []
    for a, b, xs, _ in segments(components, freqs):
        if xs == -sign:
            continue
        if spans and spans[-1][1] == a * PAIR:
            spans[-1][1] = b * PAIR
        else:
            spans.append([a * PAIR, b * PAIR])
    return [tuple(s) for s in spans]


def overlap(spans, low, high):
    cut = [(max(a, low), min(b, high)) for a, b in spans]
    return [(a, b) for a, b in cut if a < b]


def clipped(runs, low, high):
    cut = [(max(a, low // PAIR), min(b, high // PAIR), xs, ys) for a, b, xs, ys in runs]
    return [run for run in cut if run[0] < run[1]]


def south_lane(c):
    return 2 * c + 1 if 0 <= c < 8 else (32 if c < 0 else 33)


def north_lane(c):
    return 16 + 2 * c if 0 <= c < 8 else (34 if c < 0 else 35)


def lane_shift(x, source, target):
    return pltpu.roll(x, (target - source) % LANES, 1)


def lanes_of(x, index):
    return jnp.take_along_axis(x, index, axis=1, mode="promise_in_bounds")


def coefficients(coef, wide, r, xs, ys):
    rows = pl.ds(r, PAIR)

    def spread(n):
        return jnp.broadcast_to(coef[rows, n : n + 1], (PAIR, LANES))

    return dict(
        c=wide[0, rows, :],
        x=wide[1, rows, :] if xs else (spread(3), spread(4)),
        y=wide[2, rows, :] if ys else (spread(5), spread(6)),
    )


def upwind(co, xs, ys, centre, west, east, south, north):
    result = co["c"] * centre
    if xs:
        result = result + co["x"] * (west() if xs > 0 else east())
    else:
        result = result + co["x"][0] * west() + co["x"][1] * east()
    if ys:
        result = result + co["y"] * (south() if ys > 0 else north())
    else:
        result = result + co["y"][0] * south() + co["y"][1] * north()
    return result


def advect_columns(co, xs, ys, columns, state, ghost, lane):
    out = {}
    for c in columns:
        out[c] = upwind(
            co,
            xs,
            ys,
            state[c],
            lambda: state[c - 1],
            lambda: state[c + 1],
            lambda: jnp.where(
                lane == 0, lane_shift(ghost, south_lane(c), 0), pltpu.roll(state[c], 1, 1)
            ),
            lambda: jnp.where(
                lane == LANES - 1,
                lane_shift(ghost, north_lane(c), LANES - 1),
                pltpu.roll(state[c], LANES - 1, 1),
            ),
        )
    return out


def needed(columns, xs):
    want = set(columns)
    if xs >= 0:
        want |= {c - 1 for c in columns}
    if xs <= 0:
        want |= {c + 1 for c in columns}
    return sorted(want)


def over_rows(runs, body, unroll=10):
    for a, b, xs, ys in runs:
        steps = (b - a) // unroll
        if steps > 1:

            def step(p, carry, a=a, xs=xs, ys=ys):
                for j in range(unroll):
                    body(pl.multiple_of((a + p * unroll + j) * PAIR, PAIR), xs, ys)
                return carry

            lax.fori_loop(0, steps, step, 0)
            a += steps * unroll
        for p in range(a, b):
            body(p * PAIR, xs, ys)


def repeat(count, body, unroll):
    def step(p, carry):
        for j in range(unroll):
            body(p * unroll + j)
        return carry

    lax.fori_loop(0, count // unroll, step, 0)
    for p in range(count // unroll * unroll, count):
        body(p)


def bulk_of(bulk_wide, state, columns, quantities, components, bulk):
    unroll = 9

    def gather(p, totals):
        totals = list(totals)
        for j in range(unroll):
            rows = pl.ds(pl.multiple_of((p * unroll + j) * 8, 8), 8)
            wide = [bulk_wide[q, rows, :] for q in range(quantities)]
            for n, c in enumerate(columns):
                value = state[c + 2, rows, :]
                for q in range(quantities):
                    at = n * quantities + q
                    totals[at] = totals[at] + wide[q] * value
        return tuple(totals)

    zero = jnp.zeros((8, LANES), jnp.float32)
    totals = lax.fori_loop(
        0, components // 8 // unroll, gather, (zero,) * (len(columns) * quantities)
    )
    for n, c in enumerate(columns):
        for q in range(quantities):
            bulk[q, pl.ds(c, 1), :] = jnp.sum(
                totals[n * quantities + q], axis=0, keepdims=True
            )


def wave_kernel(
    spectrum, sea, transfer, coef_hbm, bulk_weight, cell_hbm, weight_hbm, u_hbm, v_hbm,
    s2_out, near_out, sides_out, far_out, cells_out, weights_out, rows_out, cols_out,
    x, a, ab, abe, t, coef, wide, bulk_turned, bulk_wide, masks, packed, turned, gturned, g, ga,
    cell, weight, u, v, cells, weights, rows_send, cols_send, cols_in,
    bulk, far_masks, acc, tl, abl, local_sem, send_sem, recv_sem, out_sem,
):
    lon, lat = lax.axis_index("lon"), lax.axis_index("lat")
    nlon, nlat = lax.axis_size("lon"), lax.axis_size("lat")
    components, width, _ = spectrum.shape
    quantities = bulk_weight.shape[0]
    runs = segments(components, NFREQ)
    plus = row_spans(components, NFREQ, 1)
    minus = row_spans(components, NFREQ, -1)
    around = [lax.rem(lon + d + nlon, nlon) for d in (-2, -1, 0, 1, 2)]
    east, west = around[3], around[1]
    has_south, has_north = lat > 0, lat < nlat - 1
    lane = lax.broadcasted_iota(jnp.int32, (PAIR, LANES), 1)

    gturned[...] = jnp.zeros_like(gturned)
    cols_in[...] = jnp.zeros_like(cols_in)

    local = []

    def load(src, dst):
        copy = pltpu.make_async_copy(src, dst, local_sem.at[len(local)])
        copy.start()
        local.append(copy)
        return copy

    barrier = pltpu.get_barrier_semaphore()

    def greet(to_lon, to_lat):
        pl.semaphore_signal(barrier, inc=1, device_id=(to_lon, to_lat), device_id_type=MESH)

    for d in (0, 1, 3, 4):
        greet(around[d], lat)

    @pl.when(has_north)
    def _():
        for d in (1, 2, 3):
            greet(around[d], lat + 1)

    @pl.when(has_south)
    def _():
        for d in (1, 2, 3):
            greet(around[d], lat - 1)

    columns_in = [load(spectrum.at[:, c, :], x.at[c + 2]) for c in range(width)]
    coef_in = load(coef_hbm, coef)
    cell_in = load(cell_hbm, cell)
    weight_in = load(weight_hbm, weight)
    u_in = load(u_hbm, u)
    v_in = load(v_hbm, v)
    transfer_in = load(transfer, t)

    pl.semaphore_wait(
        barrier, 4 + 3 * has_north.astype(jnp.int32) + 3 * has_south.astype(jnp.int32)
    )

    count = [0]

    def remote(src, dst, to_lon, to_lat):
        n = count[0]
        count[0] += 1
        return pltpu.make_async_remote_copy(
            src_ref=src,
            dst_ref=dst,
            send_sem=send_sem.at[n],
            recv_sem=recv_sem.at[n],
            device_id=(to_lon, to_lat),
            device_id_type=MESH,
        )

    def columns(spans, source, target, to_lon):
        return [
            remote(source(pl.ds(k0, k1 - k0)), target(pl.ds(k0, k1 - k0)), to_lon, lat)
            for k0, k1 in spans
        ]

    def both_ways(part, east_source, east_target, west_source, west_target):
        copies = []
        for low, high in part:
            copies += columns(overlap(plus, low, high), east_source, east_target, east)
            copies += columns(overlap(minus, low, high), west_source, west_target, west)
        return copies

    first = [
        both_ways(
            part,
            lambda k: spectrum.at[k, width - 1, :],
            lambda k: x.at[1, k, :],
            lambda k: spectrum.at[k, 0, :],
            lambda k: x.at[width + 2, k, :],
        )
        for part in (HEAD, BEHIND) + PARTS[1:]
    ]
    second = [
        both_ways(
            part,
            lambda k: a.at[width, k, :],
            lambda k: a.at[0, k, :],
            lambda k: a.at[1, k, :],
            lambda k: a.at[width + 1, k, :],
        )
        for part in PARTS
    ]
    side_masks = [
        remote(sea.at[pl.ds(width - 1, 1), :], far_masks.at[0], east, lat),
        remote(sea.at[pl.ds(0, 1), :], far_masks.at[1], west, lat),
    ]
    for copy in side_masks + first[0]:
        copy.start()

    for c in range(width):
        masks[c + 2] = jnp.broadcast_to(
            sea[pl.ds(c, 1), :].astype(jnp.float32), (PAIR, LANES)
        )

    for copy in columns_in:
        copy.wait()

    half = lane // 2
    edge_lanes = jnp.where(half < 8, LANES - 2, 0) + lane % 2

    def pack(r, values):
        total = jnp.zeros((PAIR, LANES), jnp.float32)
        for c in range(width):
            total = jnp.where(half % 8 == c, lanes_of(values[c], edge_lanes), total)
        packed[pl.ds(r, PAIR), :] = total

    def pack_rows(p):
        r = pl.multiple_of(p * PAIR, PAIR)
        values = []
        for c in range(width):
            value = x[c + 2, pl.ds(r, PAIR), :] * masks[c + 2]
            x[c + 2, pl.ds(r, PAIR), :] = value
            values.append(value)
        pack(r, values)

    repeat(components // PAIR, pack_rows, 9)
    pack(components, [masks[c + 2] for c in range(width)])
    blocks = packed.shape[0] // LANES
    tail = components + PAIR
    packed[pl.ds(tail, blocks * LANES - tail), :] = jnp.zeros(
        (blocks * LANES - tail, LANES), jnp.float32
    )
    for b in range(blocks):
        turned[:, b * LANES : (b + 1) * LANES] = jnp.transpose(
            packed[b * LANES : (b + 1) * LANES, :]
        )[:32, :]

    to_north = [
        remote(turned.at[pl.ds(0, 16), :], gturned.at[pl.ds(0, 16), :], lon, lat + 1),
        remote(turned.at[pl.ds(15, 1), :], gturned.at[pl.ds(32, 1), :], east, lat + 1),
        remote(turned.at[pl.ds(1, 1), :], gturned.at[pl.ds(33, 1), :], west, lat + 1),
    ]
    to_south = [
        remote(turned.at[pl.ds(16, 16), :], gturned.at[pl.ds(16, 16), :], lon, lat - 1),
        remote(turned.at[pl.ds(30, 1), :], gturned.at[pl.ds(34, 1), :], east, lat - 1),
        remote(turned.at[pl.ds(16, 1), :], gturned.at[pl.ds(35, 1), :], west, lat - 1),
    ]

    @pl.when(has_north)
    def _():
        for copy in to_north:
            copy.start()

    @pl.when(has_south)
    def _():
        for copy in to_south:
            copy.start()

    for copy in first[1] + first[2] + first[3]:
        copy.start()

    coef_in.wait()
    bulk_turned[...] = jnp.zeros_like(bulk_turned)
    for b in range(blocks):
        low = b * LANES
        high = min(low + LANES, components)
        bulk_turned[pl.ds(0, quantities), : high - low] = bulk_weight[:, low:high]
        part = jnp.transpose(bulk_turned[...])
        rows = pl.ds(low, high - low)
        for q in range(quantities):
            bulk_wide[q, rows, :] = jnp.broadcast_to(
                part[: high - low, q : q + 1], (high - low, LANES)
            )

    def widen(p):
        rows = pl.ds(pl.multiple_of(p * PAIR, PAIR), PAIR)
        line = coef[rows, :]
        for n in range(3):
            wide[n, rows, :] = jnp.broadcast_to(line[:, n : n + 1], (PAIR, LANES))

    repeat(components // PAIR, widen, 9)

    for copy in (cell_in, weight_in, u_in, v_in):
        copy.wait()
    height, taps, length = cell.shape
    for i in range(height):
        for tap in range(taps):
            cells[tap, pl.ds(i, 1), :] = cell[i, pl.ds(tap, 1), :]
            weights[tap, pl.ds(i, 1), :] = weight[i, pl.ds(tap, 1), :]
    levels = u.shape[0]
    for side, row in ((0, height - 1), (1, 0)):
        for level in range(levels):
            rows_send[side, pl.ds(level, 1), :] = u[level, pl.ds(row, 1), :]
            rows_send[side, pl.ds(levels + level, 1), :] = v[level, pl.ds(row, 1), :]
        for tap in range(taps):
            rows_send[side, pl.ds(2 * levels + tap, 1), :] = weights[tap, pl.ds(row, 1), :]
            rows_send[side, pl.ds(2 * levels + taps + tap, 1), :] = cells[
                tap, pl.ds(row, 1), :
            ].astype(jnp.float32)
    lane_all = lax.broadcasted_iota(jnp.int32, (height, LANES), 1)
    for side, start, source in ((0, length - LANES, LANES - 1), (1, 0, 0)):
        total = jnp.zeros((height, LANES), jnp.float32)
        for n in range(2 * levels + 2 * taps):
            if n < levels:
                block = u[n, :, start : start + LANES]
            elif n < 2 * levels:
                block = v[n - levels, :, start : start + LANES]
            elif n < 2 * levels + taps:
                block = weights[n - 2 * levels, :, start : start + LANES]
            else:
                block = cells[n - 2 * levels - taps, :, start : start + LANES].astype(jnp.float32)
            total = jnp.where(lane_all == n, lane_shift(block, source, n), total)
        cols_send[side] = total

    stores = []

    def store(src, dst):
        copy = pltpu.make_async_copy(src, dst, out_sem.at[len(stores)])
        copy.start()
        stores.append(copy)

    store(cells, cells_out)
    store(weights, weights_out)

    @pl.when(has_south)
    def _():
        for copy in to_north:
            copy.wait_recv()

    @pl.when(has_north)
    def _():
        for copy in to_south:
            copy.wait_recv()

    for b in range(blocks):
        g[b * LANES : (b + 1) * LANES, :] = jnp.transpose(
            gturned[:, b * LANES : (b + 1) * LANES]
        )
    inner = list(range(1, width - 1))
    outer = [0, width - 1]
    ghost_at = len(inner) * LANES

    def first_inner(r, xs, ys):
        co = coefficients(coef, wide, r, xs, ys)
        rows = pl.ds(r, PAIR)
        state = {c: x[c + 2, rows, :] for c in needed(inner, xs)}
        ghost = g[rows, :]
        mine = packed[rows, :]
        for c, value in advect_columns(co, xs, ys, inner, state, ghost, lane).items():
            a[c + 1, rows, :] = value
            ab[rows, (c - 1) * LANES : c * LANES] = value.astype(jnp.bfloat16)

        def sideways(step, low, high):
            moved = pltpu.roll(ghost, step % LANES, 1)
            for target, source in (low, high):
                moved = jnp.where(lane == target, lane_shift(ghost, source, target), moved)
            return moved

        value = upwind(
            co,
            xs,
            ys,
            ghost,
            lambda: sideways(2, (1, 32), (16, 34)),
            lambda: sideways(-2, (15, 33), (30, 35)),
            lambda: jnp.where(lane < 16, pltpu.roll(ghost, 1, 1), pltpu.roll(mine, 15, 1)),
            lambda: jnp.where(
                lane < 16, pltpu.roll(mine, LANES - 15, 1), pltpu.roll(ghost, LANES - 1, 1)
            ),
        )
        ga[rows, :] = value
        ab[rows, ghost_at : ghost_at + LANES] = value.astype(jnp.bfloat16)

    over_rows(runs, first_inner)
    block = 432
    ghost_mask = g[pl.ds(components, 1), :]

    def inner_product(state, shift, with_ghost, begin, end):
        def product(m, carry):
            rows = pl.ds(pl.multiple_of(m * block, PAIR), block)
            for n in range(0, len(inner), 2):
                added = jnp.dot(
                    t[rows, :],
                    ab[:, n * LANES : (n + 2) * LANES],
                    preferred_element_type=jnp.float32,
                )
                for c in (n + 1, n + 2):
                    part = added[:, (c - n - 1) * LANES : (c - n) * LANES]
                    state[c + shift, rows, :] = masks[c + 2, pl.ds(0, 1), :] * (
                        state[c + shift, rows, :] + 0.5 * part
                    )
            if with_ghost:
                added = jnp.dot(
                    t[rows, :],
                    ab[:, ghost_at : ghost_at + LANES],
                    preferred_element_type=jnp.float32,
                )
                ga[rows, :] = ghost_mask * (ga[rows, :] + 0.5 * added)
            return carry

        lax.fori_loop(begin, end, product, 0)

    def outer_part(index, advect_rows, state, shift):
        last = index == len(PARTS) - 1
        at = 0
        for low, high in PARTS[index]:
            target, moved = (abl, at - low) if last else (abe, 0)
            over_rows(
                clipped(runs, low, high), functools.partial(advect_rows, target, moved), 8
            )
            at += high - low
        for m in range(components // block):
            rows = pl.ds(m * block, block)
            if last:
                added = acc[rows, :] + jnp.dot(
                    tl[rows, :], abl[...], preferred_element_type=jnp.float32
                )
                for n, c in enumerate(outer):
                    wet = masks[c + 2, pl.ds(0, 1), :]
                    state[c + shift, rows, :] = wet * (
                        state[c + shift, rows, :] + 0.5 * added[:, n * LANES : (n + 1) * LANES]
                    )
            else:
                added = sum(
                    jnp.dot(
                        t[rows, low:high], abe[low:high, :], preferred_element_type=jnp.float32
                    )
                    for low, high in PARTS[index]
                )
                acc[rows, :] = added + acc[rows, :] if index else added

    for copy in side_masks:
        copy.wait_recv()
    for slot, side in ((1, 0), (width + 2, 1)):
        masks[slot] = jnp.broadcast_to(far_masks[side].astype(jnp.float32), (PAIR, LANES))

    def first_outer(target, moved, r, xs, ys):
        co = coefficients(coef, wide, r, xs, ys)
        rows = pl.ds(r, PAIR)
        state = {}
        for c in needed(outer, xs):
            value = x[c + 2, rows, :]
            state[c] = value * masks[c + 2] if c in (-1, width) else value
        for n, (c, value) in enumerate(
            advect_columns(co, xs, ys, outer, state, g[rows, :], lane).items()
        ):
            a[c + 1, rows, :] = value
            target[pl.ds(r + moved, PAIR), n * LANES : (n + 1) * LANES] = value.astype(
                jnp.bfloat16
            )

    transfer_in.wait()
    at = 0
    for low, high in PARTS[-1]:
        tl[:, at : at + high - low] = t[:, low:high]
        at += high - low
    inner_product(a, 1, True, 0, 2)
    for index, copies in enumerate((first[0] + first[1], first[2], first[3])):
        for copy in copies:
            copy.wait_recv()
        outer_part(index, first_outer, a, 1)
    for copies in second:
        for copy in copies:
            copy.start()
    rows_copy = [
        remote(rows_send.at[0], rows_out.at[0], east, lat),
        remote(rows_send.at[1], rows_out.at[1], west, lat),
    ]
    cols_north = remote(cols_send.at[0], cols_in.at[0], lon, lat + 1)
    cols_south = remote(cols_send.at[1], cols_in.at[1], lon, lat - 1)
    for copy in rows_copy:
        copy.start()

    @pl.when(has_north)
    def _():
        cols_north.start()

    @pl.when(has_south)
    def _():
        cols_south.start()

    inner_product(a, 1, True, 2, components // block)

    def second_step(group):
        def step(target, moved, r, xs, ys):
            co = coefficients(coef, wide, r, xs, ys)
            rows = pl.ds(r, PAIR)
            state = {c: a[c + 1, rows, :] for c in needed(group, xs)}
            for n, (c, value) in enumerate(
                advect_columns(co, xs, ys, group, state, ga[rows, :], lane).items()
            ):
                x[c + 2, rows, :] = value
                target[pl.ds(r + moved, PAIR), n * LANES : (n + 1) * LANES] = value.astype(
                    jnp.bfloat16
                )

        return step

    for copies in [side_masks] + first:
        for copy in copies:
            copy.wait_send()
    over_rows(runs, functools.partial(second_step(inner), ab, 0))
    inner_product(x, 2, False, 0, components // block)
    for c in inner:
        store(x.at[c + 2], s2_out.at[c])
    bulk_of(bulk_wide, x, inner, quantities, components, bulk)

    for index, copies in enumerate(second):
        for copy in copies:
            copy.wait_recv()
        outer_part(index, second_step(outer), x, 2)
    for c in outer:
        store(x.at[c + 2], s2_out.at[c])
    bulk_of(bulk_wide, x, outer, quantities, components, bulk)

    drift = bulk.at[pl.ds(1, 2)]
    stress = bulk.at[pl.ds(0, 2)]
    flat = [
        remote(bulk, near_out.at[2], west, lat),
        remote(bulk, near_out.at[0], east, lat),
        remote(stress, far_out.at[1], around[0], lat),
        remote(stress, far_out.at[0], around[4], lat),
    ]
    spread_north = [
        remote(drift, sides_out.at[0, 2], west, lat + 1),
        remote(drift, sides_out.at[0, 1], lon, lat + 1),
        remote(drift, sides_out.at[0, 0], east, lat + 1),
    ]
    spread_south = [
        remote(drift, sides_out.at[1, 2], west, lat - 1),
        remote(drift, sides_out.at[1, 1], lon, lat - 1),
        remote(drift, sides_out.at[1, 0], east, lat - 1),
    ]
    for copy in flat:
        copy.start()

    @pl.when(has_north)
    def _():
        for copy in spread_north:
            copy.start()

    @pl.when(has_south)
    def _():
        for copy in spread_south:
            copy.start()

    store(bulk, near_out.at[1])

    for copy in rows_copy:
        copy.wait()
    for copies in second:
        for copy in copies:
            copy.wait_send()

    @pl.when(has_north)
    def _():
        for copy in to_north + [cols_north]:
            copy.wait_send()
        cols_south.wait_recv()

    @pl.when(has_south)
    def _():
        for copy in to_south + [cols_south]:
            copy.wait_send()
        cols_north.wait_recv()

    store(cols_in, cols_out)

    for copy in flat:
        copy.wait()

    @pl.when(has_north)
    def _():
        for copy in spread_north:
            copy.wait_send()
        for copy in spread_south:
            copy.wait_recv()

    @pl.when(has_south)
    def _():
        for copy in spread_south:
            copy.wait_send()
        for copy in spread_north:
            copy.wait_recv()

    for copy in stores:
        copy.wait()


def taken_from(sources, codes, quantities):
    taken = []
    for code in codes:
        place, offset = code & (LANES - 1), code >> 9
        values = [jnp.zeros(code.shape, jnp.float32)] * len(quantities)
        for o in range(17):
            hit = offset == o
            for n, q in enumerate(quantities):
                values[n] = jnp.where(hit, lanes_of(sources(q, o), place), values[n])
        taken.append(values)
    return taken


def ocean_kernel(
    s2, u, v, sea, near, sides, far, cells, weights, rows_in, cols_in, coriolis,
    spectrum_out, u_out, v_out,
    near1, near3, sides3, forcing, edge_code, edge_weight, edge_rows, new_u, new_v, out_sem,
):
    quantities = near.shape[1]
    width = near.shape[2]
    taps, height, length = cells.shape
    levels = u.shape[0]
    writes = [
        pltpu.make_async_copy(s2.at[c], spectrum_out.at[:, c, :], out_sem.at[c])
        for c in range(width)
    ]
    for copy in writes:
        copy.start()
    for part in range(3):
        near1[:, pl.ds(8 + part * width, width), :] = near[part]
    near1[pl.ds(0, 2), pl.ds(7, 1), :] = far[0, :, pl.ds(width - 1, 1), :]
    near1[pl.ds(0, 2), pl.ds(8 + 3 * width, 1), :] = far[1, :, pl.ds(0, 1), :]
    for i in range(3 * width):
        for q in range(quantities):
            near3[q, pl.ds(3 * i, 3), :] = jnp.broadcast_to(
                near1[q, pl.ds(8 + i, 1), :], (3, LANES)
            )
        for side in range(2):
            for q in range(2):
                sides3[side, q, pl.ds(3 * i, 3), :] = jnp.broadcast_to(
                    sides[side, i // width, q, pl.ds(i % width, 1), :], (3, LANES)
                )

    def block(jb):
        lanes = pl.ds(jb * LANES, LANES)
        for i0 in range(0, height, 8):
            rows = pl.ds(i0, 8)
            taken = taken_from(
                lambda q, o: near3[q, pl.ds(i0 + 3 * o, 8), :],
                [cells[tap, rows, lanes] for tap in range(taps)],
                range(quantities),
            )
            for q in range(quantities):
                total = 0.0
                for tap in range(taps):
                    total = total + taken[tap][q] * weights[tap, rows, lanes]
                forcing[q, rows, lanes] = total
        low = lax.broadcasted_iota(jnp.int32, (8, LANES), 0) < 4
        taken = taken_from(
            lambda q, o: jnp.where(
                low,
                jnp.broadcast_to(near1[q, pl.ds(7 + o, 1), :], (8, LANES)),
                jnp.broadcast_to(near1[q, pl.ds(16 + o, 1), :], (8, LANES)),
            ),
            [edge_code[:, lanes].astype(jnp.int32)],
            range(2),
        )
        for q in range(2):
            product = taken[0][q] * edge_weight[:, lanes]
            zero = jnp.zeros_like(product)
            edge_rows[q, pl.ds(0, 1), lanes] = jnp.sum(
                jnp.where(low, product, zero), axis=0, keepdims=True
            )
            edge_rows[q, pl.ds(1, 1), lanes] = jnp.sum(
                jnp.where(low, zero, product), axis=0, keepdims=True
            )

    for side in range(2):
        edge_code[pl.ds(4 * side, 4), :] = rows_in[side, pl.ds(2 * levels + taps, taps), :]
        edge_weight[pl.ds(4 * side, 4), :] = rows_in[side, pl.ds(2 * levels, taps), :]
    blocks = length // LANES
    for jb in range(blocks):
        block(jb)

    lane = lax.broadcasted_iota(jnp.int32, (8, LANES), 1)
    here = jnp.logical_and(lane >= 2 * levels + taps, lane < 2 * levels + 2 * taps)
    edge_cols = [[], []]
    lat = lax.axis_index("lat")
    present = (lat > 0, lat < lax.axis_size("lat") - 1)
    for side in range(2):
        parts = [[], []]
        for i0 in range(0, height, 8):
            line = cols_in[side, pl.ds(i0, 8), :]
            code = jnp.where(here, line, 0.0).astype(jnp.int32)
            taken = taken_from(
                lambda q, o: sides3[side, q, pl.ds(i0 + 3 * o, 8), :], [code], range(2)
            )
            weight = jnp.where(here, pltpu.roll(line, taps, 1), 0.0)
            for q in range(2):
                value = jnp.sum(taken[0][q] * weight, axis=1, keepdims=True)
                parts[q].append(jnp.where(present[side], value, 0.0))
        for q in range(2):
            edge_cols[side].append(jnp.concatenate(parts[q], axis=0))

    row = lax.broadcasted_iota(jnp.int32, (height, length), 0)
    col = lax.broadcasted_iota(jnp.int32, (height, length), 1)

    def shifted(q, west, east, south, north):
        return (
            jnp.where(row == 0, west, pltpu.roll(q, 1, 0)),
            jnp.where(row == height - 1, east, pltpu.roll(q, height - 1, 0)),
            jnp.where(col == 0, south, pltpu.roll(q, 1, 1)),
            jnp.where(col == length - 1, north, pltpu.roll(q, length - 1, 1)),
        )

    def dx(q, index):
        low = jnp.where(row == 0, edge_rows[index, pl.ds(0, 1), :], pltpu.roll(q, 1, 0))
        high = jnp.where(
            row == height - 1, edge_rows[index, pl.ds(1, 1), :], pltpu.roll(q, height - 1, 0)
        )
        return 0.5 * (high - low)

    def dy(q, index):
        low = jnp.where(col == 0, edge_cols[0][index], pltpu.roll(q, 1, 1))
        high = jnp.where(col == length - 1, edge_cols[1][index], pltpu.roll(q, length - 1, 1))
        return 0.5 * (high - low)

    sxx, sxy, syy = forcing[0], forcing[1], forcing[2]
    force_x = -(dx(sxx, 0) + dy(sxy, 0))
    force_y = -(dx(sxy, 1) + dy(syy, 1))
    wet = sea[...].astype(jnp.float32)
    turn = jnp.broadcast_to(0.5 * coriolis[...][None], (height, length))
    for level in range(levels):
        decay = math.exp(-level / 3.0)
        here_u, here_v = u[level], v[level]

        def laplace(q, n):
            west, east, south, north = shifted(
                q,
                rows_in[0, pl.ds(n, 1), :],
                rows_in[1, pl.ds(n, 1), :],
                cols_in[0, :, n : n + 1],
                cols_in[1, :, n : n + 1],
            )
            return east + west + north + south - 4.0 * q

        new_u[level] = wet * (
            here_u
            + turn * (here_v + decay * forcing[4])
            + (0.5 * decay) * force_x
            + 0.1 * laplace(here_u, level)
        )
        new_v[level] = wet * (
            here_v
            - turn * (here_u + decay * forcing[3])
            + (0.5 * decay) * force_y
            + 0.1 * laplace(here_v, levels + level)
        )
        for n, (src, dst) in enumerate(((new_u, u_out), (new_v, v_out))):
            copy = pltpu.make_async_copy(
                src.at[level], dst.at[level], out_sem.at[width + n * levels + level]
            )
            copy.start()
            writes.append(copy)
    for copy in writes:
        copy.wait()


def local(
    spectrum,
    sea_mask,
    transfer,
    bulk_weight,
    remap_cell,
    remap_weight,
    ocean_u,
    ocean_v,
    ocean_mask,
    coriolis,
):
    f32, i32 = jnp.float32, jnp.int32
    components, width, _ = spectrum.shape
    levels, height, length = ocean_u.shape
    taps = remap_cell.shape[2]
    quantities = bulk_weight.shape[0]
    padded = -(-(components + PAIR) // LANES) * LANES
    coef = courant(components, NFREQ)
    cell = jnp.transpose(remap_cell, (0, 2, 1))
    weight = jnp.transpose(remap_weight, (0, 2, 1))
    messages = 2 * levels + 2 * taps
    S = jax.ShapeDtypeStruct
    dma = pltpu.SemaphoreType.DMA
    near_shape = (3, quantities, width, LANES)
    sides_shape = (2, 3, 2, width, LANES)
    far_shape = (2, 2, width, LANES)
    s2, near, sides, far, cells, weights, rows_in, cols_in = pl.pallas_call(
        wave_kernel,
        name="wave",
        out_shape=(
            S((width, components, LANES), f32),
            S(near_shape, f32),
            S(sides_shape, f32),
            S(far_shape, f32),
            S((taps, height, length), i32),
            S((taps, height, length), f32),
            S((2, messages, length), f32),
            S((2, height, LANES), f32),
        ),
        in_specs=[HBM, VMEM, HBM, HBM, VMEM, HBM, HBM, HBM, HBM],
        out_specs=(ANY,) * 8,
        scratch_shapes=[
            pltpu.VMEM((width + 4, components, LANES), f32),
            pltpu.VMEM((width + 2, components, LANES), f32),
            pltpu.VMEM((components, (width - 1) * LANES), jnp.bfloat16),
            pltpu.VMEM((components, 2 * LANES), jnp.bfloat16),
            pltpu.VMEM((components, components), jnp.bfloat16),
            pltpu.VMEM((components, 8), f32),
            pltpu.VMEM((3, components, LANES), f32),
            pltpu.VMEM((LANES, LANES), f32),
            pltpu.VMEM((quantities, components, LANES), f32),
            pltpu.VMEM((width + 4, PAIR, LANES), f32),
            pltpu.VMEM((padded, LANES), f32),
            pltpu.VMEM((32, padded), f32),
            pltpu.VMEM((LANES, padded), f32),
            pltpu.VMEM((padded, LANES), f32),
            pltpu.VMEM((components, LANES), f32),
            pltpu.VMEM((height, taps, length), i32),
            pltpu.VMEM((height, taps, length), f32),
            pltpu.VMEM((levels, height, length), f32),
            pltpu.VMEM((levels, height, length), f32),
            pltpu.VMEM((taps, height, length), i32),
            pltpu.VMEM((taps, height, length), f32),
            pltpu.VMEM((2, messages, length), f32),
            pltpu.VMEM((2, height, LANES), f32),
            pltpu.VMEM((2, height, LANES), f32),
            pltpu.VMEM((quantities, width, LANES), f32),
            pltpu.VMEM((2, 1, LANES), i32),
            pltpu.VMEM((components, 2 * LANES), f32),
            pltpu.VMEM((components, LAST), jnp.bfloat16),
            pltpu.VMEM((LAST, 2 * LANES), jnp.bfloat16),
            dma((16,)),
            dma((44,)),
            dma((44,)),
            dma((16,)),
        ],
        compiler_params=pltpu.CompilerParams(
            collective_id=0, has_side_effects=True, vmem_limit_bytes=WAVE_GRANT
        ),
    )(
        *map(
            in_hbm,
            (
                spectrum, sea_mask, transfer, jnp.asarray(coef), bulk_weight, cell, weight,
                ocean_u, ocean_v,
            ),
        )
    )

    return pl.pallas_call(
        ocean_kernel,
        name="ocean",
        out_shape=(S(spectrum.shape, f32), S(ocean_u.shape, f32), S(ocean_v.shape, f32)),
        in_specs=[ANY] + [VMEM] * 11,
        out_specs=(HBM, HBM, HBM),
        scratch_shapes=[
            pltpu.VMEM((quantities, 8 + 3 * width + 8, LANES), f32),
            pltpu.VMEM((quantities, 9 * width, LANES), f32),
            pltpu.VMEM((2, 2, 9 * width, LANES), f32),
            pltpu.VMEM((quantities, height, length), f32),
            pltpu.VMEM((8, length), f32),
            pltpu.VMEM((8, length), f32),
            pltpu.VMEM((2, 8, length), f32),
            pltpu.VMEM(ocean_u.shape, f32),
            pltpu.VMEM(ocean_v.shape, f32),
            dma((width + 2 * levels,)),
        ],
        compiler_params=pltpu.CompilerParams(vmem_limit_bytes=OCEAN_GRANT),
    )(
        s2, ocean_u, ocean_v, ocean_mask, near, sides, far, cells, weights, rows_in, cols_in,
        coriolis,
    )


def solution(mesh):
    placed = (
        P(None, "lon", "lat"),
        P("lon", "lat"),
        P(),
        P(),
        P("lon", "lat", None),
        P("lon", "lat", None),
        P(None, "lon", "lat"),
        P(None, "lon", "lat"),
        P("lon", "lat"),
        P("lat"),
    )
    return jax.shard_map(
        local,
        mesh=mesh,
        in_specs=placed,
        out_specs=(P(None, "lon", "lat"), P(None, "lon", "lat"), P(None, "lon", "lat")),
        check_vma=False,
    )
```
